512 devices in a mesh: patch: 128 (over z, y, core), visit: 4 (over x).
Axes of the slice: x: 4, y: 4, z: 16, core: 2. Of those that a mesh axis runs over, the one named last changes fastest.
Arguments:
- science: float32 [65536, 2, 128], P(('patch', 'visit')), may hold values from -40 to 40
- inverse_sigma: float32 [65536, 2, 128], P(('patch', 'visit')), may hold values from 0.24 to 3.6
- template: float32 [128, 256, 1024], P('patch', 'visit'), may hold values from -6 to 6
- destination: int32 [65536], P(('patch', 'visit')), may hold values from 0 to 127, as said below
- offsets: int32 [65536, 2], P(('patch', 'visit')), may hold values from 0 to 876, as said below
- visit_local: int32 [65536], P(('patch', 'visit')), may hold values from 0 to 15, as said below
Outputs:
- difference: float32 [65536, 2, 128], P(('patch', 'visit'))
- coefficients: float32 [64, 28], P('visit')
The draws below stay inside these ranges and needn't reach their ends.
Inputs may be any that keep to these rules, and one draw needn't show every extreme that they name: `destination`: in each aligned block of 128 rows no patch is named more than 2 times, and in every draw some patch is named exactly 2 times in every block. `offsets`: column 0 is at most 234, column 1 at most 876. `visit_local`: each aligned block of 128 rows holds every value exactly 128 // 16 times.
All inputs are finite; a program needn't handle non-finite values.
Results may differ from the reference program's by a relative error of at most 0.0098.
Values may be sent and summed in bfloat16 or wider, within the bound.
No kernel may reach another device: no remote copies, remote signals or barrier semaphores. Data moves between devices by JAX's collectives and lax.ppermute only.
A program may use at most 64 MiB of HBM per device.

```python
import math
import jax
import jax.numpy as jnp
import numpy as np
from jax import lax

KR = 10
NF = 11
NB = 28
TR = 2
TC = 128
PR = 256
PC = 1024
VIS_DEV = 16
TILES_DEV = 128
HOLDER_TILE_MAX = 2
VISITS = 64
TILES = 65536
N_PATCH = 128
N_VISIT = 4


def holder_arrangement(key):
    holders = N_PATCH * N_VISIT
    slot_grand_count = N_PATCH * HOLDER_TILE_MAX
    hot_total = max(1, N_PATCH // 8)
    ranking = jax.random.permutation(jax.random.fold_in(key, 101), N_PATCH)
    busy_indicator = jnp.where(ranking < hot_total, 1, 0).astype(jnp.int32)
    slot_ids = jnp.arange(slot_grand_count, dtype=jnp.int32)
    extra_credit = jnp.repeat(busy_indicator, HOLDER_TILE_MAX, total_repeat_length=slot_grand_count) * 65536

    def one_holder(holder_key):
        rating_sort_key, shuffle_key, visit_key, row_key, column_key = jax.random.split(holder_key, 5)
        priority_rating = jax.random.randint(rating_sort_key, (slot_grand_count,), 0, 65536, dtype=jnp.int32) + extra_credit
        keyed = priority_rating * slot_grand_count + slot_ids
        chosen = jnp.argsort(-keyed)[:TILES_DEV].astype(jnp.int32)
        placed = jax.random.permutation(shuffle_key, chosen)
        visits = jax.random.permutation(visit_key, jnp.arange(TILES_DEV, dtype=jnp.int32) % VIS_DEV)
        row_starts = jax.random.randint(row_key, (TILES_DEV,), 0, PR - TR - 2 * KR + 1, dtype=jnp.int32)
        column_starts = jax.random.randint(column_key, (TILES_DEV,), 0, PC - TC - 2 * KR + 1, dtype=jnp.int32)
        return (placed // HOLDER_TILE_MAX, visits, jnp.stack([row_starts, column_starts], axis=1))
    holder_keys = jax.random.split(jax.random.fold_in(key, 202), holders)
    patch_ids, visits, starts = jax.vmap(one_holder)(holder_keys)
    return (patch_ids.reshape(TILES), visits.reshape(TILES), starts.reshape(TILES, 2))


def template_field(key):
    base_key = jax.random.fold_in(key, 303)
    first_key = jax.random.fold_in(base_key, 0)
    return jnp.clip(jax.random.normal(first_key, (N_PATCH, PR, PC)), -6.0, 6.0)


def sigma_field(key):
    level_key, pixel_key = jax.random.split(jax.random.fold_in(key, 505))
    level_scale = jnp.exp(jax.random.uniform(level_key, (TILES, 1, 1), minval=math.log(0.3), maxval=math.log(3.0)))
    return level_scale * jax.random.uniform(pixel_key, (TILES, TR, TC), minval=0.8, maxval=1.2)


def draw_destination(key, part):
    patch_ids, visits, starts = holder_arrangement(key)
    return patch_ids


def draw_visit_local(key, part):
    patch_ids, visits, starts = holder_arrangement(key)
    return visits


def draw_offsets(key, part):
    patch_ids, visits, starts = holder_arrangement(key)
    return starts


def draw_template(key, part):
    return template_field(key).astype(jnp.float32)


def draw_inverse_sigma(key, part):
    return sigma_field(key).astype(jnp.float32)


def draw_science(key, part):
    patch_ids, visits, starts = holder_arrangement(key)
    field = template_field(key)
    inverse = sigma_field(key)
    tile_ids = jnp.arange(TILES, dtype=jnp.int32)
    global_visit = tile_ids // TILES_DEV % N_VISIT * VIS_DEV + visits
    kernel_key, noise_key = jax.random.split(jax.random.fold_in(key, 404))
    center = jnp.zeros((3, 3), jnp.float32).at[1, 1].set(1.0)
    kernels = 0.25 * jax.random.normal(kernel_key, (VISITS, 3, 3)) + center[None]
    reach = KR - 1
    span_count = 2 * reach + 1
    width_key, strength_key = jax.random.split(jax.random.fold_in(key, 606))
    broad_widths = KR * jax.random.uniform(width_key, (VISITS, 1), minval=0.25, maxval=0.4)
    broad_strengths = jax.random.uniform(strength_key, (VISITS, 1), minval=0.8, maxval=1.2)
    tap_points = jnp.arange(-reach, reach + 1, dtype=jnp.float32)[None, :]
    bells = jnp.exp(-tap_points * tap_points / (2.0 * broad_widths * broad_widths))
    bells = bells * jnp.sqrt(broad_strengths / jnp.sum(bells * bells, axis=1, keepdims=True))
    amplitude = 1.0 + 2.0 * patch_ids.astype(jnp.float32) / max(N_PATCH - 1, 1)

    def one_tile(patch_id, start_pair, weights_three, bell_taps, scale_value):
        patch_field = lax.dynamic_index_in_dim(field, patch_id, 0, keepdims=False)
        window = lax.dynamic_slice(patch_field, (start_pair[0] + KR - 1, start_pair[1] + KR - 1), (TR + 2, TC + 2))
        running_sum = jnp.zeros((TR, TC), jnp.float32)
        for row_shift in range(3):
            for col_shift in range(3):
                running_sum = running_sum + weights_three[row_shift, col_shift] * window[row_shift:row_shift + TR, col_shift:col_shift + TC]
        wide_window = lax.dynamic_slice(patch_field, (start_pair[0] + KR - reach, start_pair[1] + KR - reach), (TR + 2 * reach, TC + 2 * reach))
        row_pass = jnp.zeros((TR, TC + 2 * reach), jnp.float32)
        for row_shift in range(span_count):
            row_pass = row_pass + bell_taps[row_shift] * wide_window[row_shift:row_shift + TR, :]
        broad_part = jnp.zeros((TR, TC), jnp.float32)
        for col_shift in range(span_count):
            broad_part = broad_part + bell_taps[col_shift] * row_pass[:, col_shift:col_shift + TC]
        return scale_value * (running_sum + broad_part)
    block_size = TILES_DEV * N_VISIT
    block_count = TILES // block_size

    def shaped(values):
        return values.reshape((block_count, block_size) + values.shape[1:])
    truth = lax.map(lambda pieces: jax.vmap(one_tile)(pieces[0], pieces[1], pieces[2], pieces[3], pieces[4]), (shaped(patch_ids), shaped(starts), shaped(kernels[global_visit]), shaped(bells[global_visit]), shaped(amplitude)))
    truth = truth.reshape(TILES, TR, TC)
    noise = jax.random.normal(noise_key, (TILES, TR, TC))
    return jnp.clip(truth + 0.3 * noise / inverse, -40.0, 40.0).astype(jnp.float32)


def setup_inputs(seed: int = 0) -> dict:
    keys = jax.random.split(jax.random.key(seed), 7)
    science = draw_science(jax.random.fold_in(keys[6], 71), 0)
    inverse_sigma = draw_inverse_sigma(jax.random.fold_in(keys[6], 71), 0)
    template = draw_template(jax.random.fold_in(keys[6], 71), 0)
    destination = draw_destination(jax.random.fold_in(keys[6], 71), 0)
    offsets = draw_offsets(jax.random.fold_in(keys[6], 71), 0)
    visit_local = draw_visit_local(jax.random.fold_in(keys[6], 71), 0)
    return {"science": science, "inverse_sigma": inverse_sigma, "template": template, "destination": destination, "offsets": offsets, "visit_local": visit_local}


gauss_widths = (1.0, 2.0, 4.0)
poly_degrees = (4, 2, 2)

def filter_table(radius):
    tap_points = np.arange(-radius, radius + 1) * 1.0
    raw_columns = []
    for width_value, degree in zip(gauss_widths, poly_degrees):
        bell_curve = np.exp(-tap_points * tap_points / (2.0 * width_value * width_value))
        for power_index in range(degree + 1):
            raw_columns.append(bell_curve * (tap_points / radius) ** power_index)
    orthonormal = []
    for column in raw_columns:
        vector = column.copy()
        for repeat_index in range(2):
            for earlier in orthonormal:
                vector = vector - np.dot(earlier, vector) * earlier
        orthonormal.append(vector / np.sqrt(np.dot(vector, vector)))
    return np.stack(orthonormal, axis=1).astype(np.float32)

def pair_layout():
    column_ids = []
    row_ids = []
    filter_runs = []
    offset = 0
    for degree in poly_degrees:
        for first_index in range(degree + 1):
            filter_runs.append((offset + first_index, offset, offset + degree - first_index + 1))
            for second_index in range(degree + 1 - first_index):
                column_ids.append(offset + first_index)
                row_ids.append(offset + second_index)
        offset += degree + 1
    return (column_ids, row_ids, filter_runs)

def rounded(values):
    return lax.optimization_barrier(values.astype(jnp.bfloat16)).astype(jnp.float32)

def reference(science, inverse_sigma, template, destination, offsets, visit_local):
    column_ids, row_ids, filter_runs = pair_layout()
    taps_count = 2 * KR + 1
    filter_values = rounded(jnp.asarray(filter_table(KR)).astype(jnp.float32))
    column_index = jnp.asarray(column_ids, dtype=jnp.int32)
    row_index = jnp.asarray(row_ids, dtype=jnp.int32)
    template_round = rounded(template)
    weights = rounded(inverse_sigma)
    scaled_science = rounded(science * inverse_sigma)
    tile_ids = jnp.arange(TILES, dtype=jnp.int32)
    visit_of = tile_ids // TILES_DEV % N_VISIT * VIS_DEV + visit_local
    height = TR + 2 * KR
    breadth = TC + 2 * KR
    block_size = TILES_DEV * N_VISIT
    block_count = TILES // block_size
    highest = lax.Precision.HIGHEST

    def cut_window(patch_id, row_at, column_at):
        starts = (patch_id.astype(jnp.int32), row_at.astype(jnp.int32), column_at.astype(jnp.int32))
        return lax.dynamic_slice(template_round, starts, (1, height, breadth))[0]

    def filtered_of(windows):
        running_sum = windows[:, None, 0:TR, :] * filter_values[0][None, :, None, None]
        for shift_index in range(1, taps_count):
            running_sum = running_sum + windows[:, None, shift_index:shift_index + TR, :] * filter_values[shift_index][None, :, None, None]
        return rounded(running_sum)

    def images_of(filtered):
        chosen = filtered[:, row_index]
        column_weights = filter_values[:, column_index]
        running_sum = chosen[..., 0:TC] * column_weights[0][None, :, None, None]
        for shift_index in range(1, taps_count):
            running_sum = running_sum + chosen[..., shift_index:shift_index + TC] * column_weights[shift_index][None, :, None, None]
        return running_sum

    def shaped(values):
        return values.reshape((block_count, block_size) + values.shape[1:])

    def windows_of(patch_ids, offset_rows):
        return jax.vmap(cut_window)(patch_ids, offset_rows[:, 0], offset_rows[:, 1])

    def first_pass(carry, pieces):
        gram_sum, right_sum = carry
        patch_ids, offset_rows, block_visits, block_weights, block_scaled = pieces
        images = images_of(filtered_of(windows_of(patch_ids, offset_rows)))
        design = rounded(images * block_weights[:, None])
        design = jnp.concatenate([design, block_weights[:, None]], axis=1).reshape(block_size, NB, TR * TC)
        gram_matrix = jnp.einsum('nkp,nlp->nkl', design, design, precision=highest)
        right_vector = jnp.einsum('nkp,np->nk', design, block_scaled.reshape(block_size, TR * TC), precision=highest)
        gram_sum = gram_sum + jax.ops.segment_sum(gram_matrix, block_visits, num_segments=VISITS)
        right_sum = right_sum + jax.ops.segment_sum(right_vector, block_visits, num_segments=VISITS)
        return ((gram_sum, right_sum), None)
    start = (jnp.zeros((VISITS, NB, NB), jnp.float32), jnp.zeros((VISITS, NB), jnp.float32))
    (gram_total, right_total), unused = lax.scan(first_pass, start, (shaped(destination), shaped(offsets), shaped(visit_of), shaped(weights), shaped(scaled_science)))
    coefficients = jnp.linalg.solve(gram_total, right_total[..., None])[..., 0]
    mixing = jnp.zeros((VISITS, NF, NF), jnp.float32).at[:, column_index, row_index].set(coefficients[:, :NB - 1])

    def second_pass(pieces):
        patch_ids, offset_rows, block_visits, block_science = pieces
        filtered = filtered_of(windows_of(patch_ids, offset_rows))
        combined = jnp.einsum('nab,nbix->naix', mixing[block_visits], filtered, precision=highest)
        running_sum = jnp.einsum('a,naij->nij', filter_values[0], combined[..., 0:TC], precision=highest)
        for shift_index in range(1, taps_count):
            running_sum = running_sum + jnp.einsum('a,naij->nij', filter_values[shift_index], combined[..., shift_index:shift_index + TC], precision=highest)
        model = rounded(running_sum + coefficients[block_visits, NB - 1][:, None, None])
        return block_science - model
    difference = lax.map(second_pass, (shaped(destination), shaped(offsets), shaped(visit_of), shaped(science)))
    return (difference.reshape(TILES, TR, TC), coefficients)
```

```python
import functools

import jax
import jax.numpy as jnp
import numpy as np
from jax import lax
from jax.experimental import pallas as pl
from jax.experimental.pallas import tpu as pltpu
from jax.sharding import PartitionSpec as P

KR = 10
TAPS = 2 * KR + 1
NB = 28
VIS_DEV = 16
ROWS = 32
LANES = 128
GROUP = 8
SLOT_ROWS = 10

gauss_widths = (1.0, 2.0, 4.0)
poly_degrees = (4, 2, 2)

SET_P = (0, 1, 2, 3, 4, 5, 6, 7)
SET_Q = (8, 9, 10, 0, 1, 0, 8, 9)
COLS_P = (0, 1, 2, 5, 6, 7)
COLS_Q = (8, 3, 4, 9, 10)

ROW_PAIRS = (
    [(0, b) for b in range(5)] + [(5, 5), (5, 6), (5, 7)]
    + [(1, b) for b in range(4)] + [None, (6, 5), (6, 6), None]
    + [(2, 0), (2, 1), (2, 2), None, None, (7, 5), (10, 8), None]
    + [(8, 8), (8, 9), (8, 10), (3, 0), (3, 1), (4, 0), (9, 8), (9, 9)]
)
WEIGHT_ROW = 12
SCIENCE_ROW = 15


def filter_table(radius):
    tap_points = np.arange(-radius, radius + 1) * 1.0
    raw_columns = []
    for width_value, degree in zip(gauss_widths, poly_degrees):
        bell_curve = np.exp(-tap_points * tap_points / (2.0 * width_value * width_value))
        for power_index in range(degree + 1):
            raw_columns.append(bell_curve * (tap_points / radius) ** power_index)
    orthonormal = []
    for column in raw_columns:
        vector = column.copy()
        for repeat_index in range(2):
            for earlier in orthonormal:
                vector = vector - np.dot(earlier, vector) * earlier
        orthonormal.append(vector / np.sqrt(np.dot(vector, vector)))
    return np.stack(orthonormal, axis=1).astype(np.float32)


def basis_rows():
    rows = []
    offset = 0
    for degree in poly_degrees:
        for first in range(degree + 1):
            for second in range(degree + 1 - first):
                rows.append(ROW_PAIRS.index((offset + first, offset + second)))
        offset += degree + 1
    return rows + [WEIGHT_ROW]


def constants():
    values = filter_table(KR)
    band = np.zeros((256, 48), np.float32)
    for which, held in enumerate((SET_P, SET_Q)):
        for y in range(16):
            for row, b in enumerate(held):
                band[which * 128 + y * 8 + row, y : y + TAPS] = values[:, b]
    columns = []
    for held in (COLS_P, COLS_Q):
        wide = np.zeros((256, len(held) * LANES), np.float32)
        for place, a in enumerate(held):
            for j in range(LANES):
                wide[j : j + TAPS, place * LANES + j] = values[:, a]
        columns.append(wide)
    return [jnp.asarray(c).astype(jnp.bfloat16) for c in (band, *columns)]


def iota(shape, axis):
    return lax.broadcasted_iota(jnp.int32, shape, axis)


def pack_kernel(science, sigma, dest, visit, offsets, packed, slots, stack):
    d = jnp.broadcast_to(dest[...], (LANES, LANES))
    earlier = (d.T == d) & (iota(d.shape, 0) < iota(d.shape, 1))
    rank = jnp.sum(jnp.where(earlier, 1, 0), axis=0, keepdims=True)
    slots[...] = jnp.broadcast_to(dest[...] * 2 + rank, slots.shape)
    for i in range(2):
        weight = sigma[pl.ds(i, LANES, stride=2), :]
        scaled = science[pl.ds(i, LANES, stride=2), :] * weight
        stack[i * LANES : (i + 1) * LANES, :] = scaled.astype(jnp.bfloat16)
        stack[(2 + i) * LANES : (3 + i) * LANES, :] = weight.astype(jnp.bfloat16)
    column = offsets[1:2, :]
    fields = (visit[...], offsets[0:1, :], column >> 7, column & 127)
    row = iota((LANES, LANES), 0)
    details = jnp.zeros((LANES, LANES), jnp.float32)
    for place, field in enumerate(fields):
        details = jnp.where(row == place, field.astype(jnp.float32), details)
    stack[4 * LANES :, :] = details.T.astype(jnp.bfloat16)
    first = dest[...] * SLOT_ROWS
    targets = (first + 2 * rank, first + 2 * rank + 1, first + 4 + 2 * rank,
               first + 5 + 2 * rank, first + 8 + rank)
    target = jnp.concatenate(targets, axis=1)
    block = 256
    for start in range(0, packed.shape[0], block):
        chosen = iota((block, 5 * LANES), 0) + start == target
        chosen = jnp.where(chosen, 1.0, 0.0).astype(jnp.bfloat16)
        packed[start : start + block, :] = jnp.dot(
            chosen, stack[...], preferred_element_type=jnp.float32
        ).astype(jnp.bfloat16)


def fit_kernel(arrived, template, band, wide_p, wide_q, images, gram, details_out,
               rows_p, rows_q, data, left_p, left_q, right_p, right_q, design,
               total, details, sem):
    data[...] = arrived[...].astype(jnp.float32)
    for c in range(2):
        fields = data[pl.ds(8 + c, LANES, stride=SLOT_ROWS), :].T
        details_out[c] = fields[0:8, :].astype(jnp.int32)
    copy = pltpu.make_async_copy(details_out, details, sem)
    copy.start()
    for y in range(0, 240, 16):
        depth = min(48, 256 - y)
        made = jnp.dot(band[:, 0:depth], template[y : y + depth, :],
                       preferred_element_type=jnp.float32)
        made = made.astype(jnp.bfloat16).astype(jnp.float32)
        rows_p[y * 8 : y * 8 + 128, :] = made[0:128]
        rows_q[y * 8 : y * 8 + 128, :] = made[128:256]
    total[...] = jnp.zeros_like(total)
    copy.wait()
    lane = iota((16, LANES), 1)
    sub = iota((8, LANES), 0)
    quarter = iota((ROWS, LANES), 1) >> 5

    def step(g, carry):
        for t in range(GROUP):
            c = t % 2
            src = g * (GROUP // 2) + t // 2
            r = details[c, 1, src]
            q = details[c, 2, src]
            s = details[c, 3, src]
            back = (LANES - s) & 127
            keep = lane < LANES - s
            for rows, left in ((rows_p, left_p), (rows_q, left_q)):
                turned = []
                for m in range(3):
                    at = pl.multiple_of(jnp.minimum(q + m, 7) * LANES, LANES)
                    piece = rows[pl.ds(pl.multiple_of(r * 8, 8), 16), pl.ds(at, LANES)]
                    turned.append(pltpu.roll(piece, back, 1))
                for m in range(2):
                    left[t * 16 : t * 16 + 16, m * LANES : (m + 1) * LANES] = jnp.where(
                        keep, turned[m], turned[m + 1]
                    ).astype(jnp.bfloat16)
        right_p[...] = jnp.dot(left_p[...], wide_p[...], preferred_element_type=jnp.float32)
        right_q[...] = jnp.dot(left_q[...], wide_q[...], preferred_element_type=jnp.float32)
        for t in range(GROUP):
            c = t % 2
            src = g * (GROUP // 2) + t // 2
            for i in range(2):
                at = t * 16 + i * 8

                def p(a):
                    k = COLS_P.index(a)
                    return right_p[at : at + 8, k * LANES : (k + 1) * LANES]

                def q(a):
                    k = COLS_Q.index(a)
                    return right_q[at : at + 8, k * LANES : (k + 1) * LANES]

                v0 = jnp.where(sub < 5, p(0), p(5))
                v1 = jnp.where(sub < 4, p(1), jnp.where(sub == 7, 0.0, p(6)))
                v1 = jnp.where(sub == 4, 1.0, v1)
                v2 = jnp.where(sub < 3, p(2), jnp.where(sub == 5, p(7), jnp.where(sub == 6, q(10), 0.0)))
                v3 = jnp.where(sub < 3, q(8), jnp.where(sub < 5, q(3), jnp.where(sub < 6, q(4), q(9))))
                lanes = slice(i * LANES, (i + 1) * LANES)
                first = pl.multiple_of((g * GROUP + t) * ROWS, ROWS)
                for m, v in enumerate((v0, v1, v2, v3)):
                    images[pl.ds(first + 8 * m, 8), lanes] = v
                weight = data[pl.ds(src * SLOT_ROWS + 4 + 2 * c + i, 1), :]
                science = data[pl.ds(src * SLOT_ROWS + 2 * c + i, 1), :]
                d1 = jnp.where(sub == 7, science, v1 * weight)
                whole = jnp.concatenate([v0 * weight, d1, v2 * weight, v3 * weight], axis=0)
                design[t * ROWS : (t + 1) * ROWS, lanes] = whole.astype(jnp.bfloat16)
        for h in range(GROUP // 4):
            part = design[h * 128 : (h + 1) * 128, :]
            product = lax.dot_general(part, part, (((1,), (1,)), ((), ())),
                                      preferred_element_type=jnp.float32)
            for n in range(4):
                t = h * 4 + n
                v = details[t % 2, 0, g * (GROUP // 2) + t // 2]
                total[v] += jnp.where(quarter == n, product[n * ROWS : (n + 1) * ROWS, :], 0.0)
        return carry

    lax.fori_loop(0, 2 * LANES // GROUP, step, 0)
    lane8 = iota((8, LANES), 1) >> 5
    for v in range(VIS_DEV):
        whole = total[v]
        whole = whole + pltpu.roll(whole, 64, 1)
        whole = whole + pltpu.roll(whole, 32, 1)
        low = jnp.where(lane8 == 0, whole[0:8], whole[8:16])
        high = jnp.where(lane8 == 2, whole[16:24], whole[24:32])
        gram[v * 8 : v * 8 + 8, :] = jnp.where(lane8 < 2, low, high)


def middle_kernel(parts, out):
    whole = parts[0]
    for n in range(1, parts.shape[0]):
        whole = whole + parts[n]
    for n in range(out.shape[0]):
        out[n] = whole


def solve_kernel(parts, out):
    whole = parts[0]
    for n in range(1, parts.shape[0]):
        whole = whole + parts[n]
    lane8 = iota((8, LANES), 1) >> 5
    pieces = []
    for p in range(4):
        piece = jnp.zeros((8, LANES), jnp.float32)
        for h in range(2):
            turned = whole[h * 8 : h * 8 + 8]
            shift = (32 * h - 32 * p) % LANES
            if shift:
                turned = pltpu.roll(turned, shift, 1)
            piece = jnp.where(lane8 == h, turned, piece)
        pieces.append(piece)
    matrix = jnp.concatenate(pieces, axis=0)
    lane = iota((ROWS, LANES), 1)
    row_lane = iota((1, LANES), 1)
    half = lane < 32
    for k in basis_rows():
        row = matrix[k : k + 1, :]
        column = jnp.where(half, matrix[:, k : k + 1], matrix[:, 32 + k : 33 + k])
        pivot = jnp.broadcast_to(column[k : k + 1, :], (ROWS, LANES))
        scaled = column / pivot
        matrix = jnp.where((lane & 31) == k, scaled, matrix - scaled * row)
    answer = matrix[SCIENCE_ROW : SCIENCE_ROW + 1, :]
    valid = row_lane < 0
    for k in basis_rows():
        valid = valid | ((row_lane & 31) == k)
    answer = jnp.where(valid & (row_lane < 64), answer, 0.0)
    for n in range(out.shape[0]):
        out[n] = answer


def model_kernel(details, answers, images, model, wide, sums):
    block = images.shape[0] // ROWS
    g = pl.program_id(0)

    @pl.when(g == 0)
    def _():
        turned = jnp.concatenate([answers[...], jnp.zeros((LANES - 8, LANES), jnp.float32)], axis=0).T
        for v in range(VIS_DEV):
            piece = turned[(v % 2) * ROWS : (v % 2) * ROWS + ROWS, v // 2 : v // 2 + 1]
            wide[v] = jnp.broadcast_to(piece, (ROWS, LANES))

    for t in range(block):
        v = details[t % 2, 0, g * (block // 2) + t // 2]
        for i in range(2):
            lanes = slice(i * LANES, (i + 1) * LANES)
            acc = wide[v, 0:8] * images[t * ROWS : t * ROWS + 8, lanes]
            for m in range(1, 4):
                acc = acc + wide[v, 8 * m : 8 * m + 8] * images[t * ROWS + 8 * m : t * ROWS + 8 * m + 8, lanes]
            sums[(2 * t + i) * 8 : (2 * t + i) * 8 + 8, :] = acc
    out = sums[pl.ds(0, 2 * block, stride=8), :]
    for n in range(1, 8):
        out = out + sums[pl.ds(n, 2 * block, stride=8), :]
    model[...] = out.astype(jnp.bfloat16)


def final_kernel(slots, science, returned, out):
    column = jnp.broadcast_to(slots[0:1, :], (LANES, LANES)).T
    column = jnp.concatenate([column] * 4, axis=1)
    for i in range(2):
        chosen = iota((LANES, 4 * LANES), 1) == column * 2 + i
        chosen = jnp.where(chosen, 1.0, 0.0).astype(jnp.bfloat16)
        model = jnp.dot(chosen, returned[...], preferred_element_type=jnp.float32)
        out[pl.ds(i, LANES, stride=2), :] = science[pl.ds(i, LANES, stride=2), :] - model


def vmem(count):
    return [pl.BlockSpec(memory_space=pltpu.VMEM)] * count


def shape(dims, dtype=jnp.float32):
    return jax.ShapeDtypeStruct(dims, dtype)


def params(**more):
    return pltpu.CompilerParams(vmem_limit_bytes=60 << 20, **more)


def pack(science, sigma, dest, visit, offsets):
    return pl.pallas_call(
        pack_kernel,
        out_shape=(shape((LANES * SLOT_ROWS, LANES), jnp.bfloat16), shape((8, LANES), jnp.int32)),
        in_specs=vmem(5), out_specs=tuple(vmem(2)),
        scratch_shapes=[pltpu.VMEM((5 * LANES, LANES), jnp.bfloat16)],
        compiler_params=params(), name="pack",
    )(science, sigma, dest, visit, offsets)


def fit(arrived, template, band, wide_p, wide_q):
    return pl.pallas_call(
        fit_kernel,
        out_shape=(shape((2 * LANES * ROWS, 2 * LANES)), shape((VIS_DEV * 8, LANES)),
                   shape((2, 8, LANES), jnp.int32)),
        in_specs=vmem(5), out_specs=tuple(vmem(3)),
        scratch_shapes=[
            pltpu.VMEM((1920, 1024), jnp.float32), pltpu.VMEM((1920, 1024), jnp.float32),
            pltpu.VMEM((LANES * SLOT_ROWS, LANES), jnp.float32),
            pltpu.VMEM((GROUP * 16, 256), jnp.bfloat16), pltpu.VMEM((GROUP * 16, 256), jnp.bfloat16),
            pltpu.VMEM((GROUP * 16, len(COLS_P) * LANES), jnp.float32),
            pltpu.VMEM((GROUP * 16, len(COLS_Q) * LANES), jnp.float32),
            pltpu.VMEM((GROUP * ROWS, 256), jnp.bfloat16),
            pltpu.VMEM((VIS_DEV, ROWS, LANES), jnp.float32),
            pltpu.SMEM((2, 8, LANES), jnp.int32), pltpu.SemaphoreType.DMA,
        ],
        compiler_params=params(), name="fit",
    )(arrived, template, band, wide_p, wide_q)


def middle(parts):
    return pl.pallas_call(middle_kernel, out_shape=shape((16,) + parts.shape[1:]),
                          in_specs=vmem(1), out_specs=vmem(1)[0], name="middle")(parts)


def solve(parts):
    return pl.pallas_call(solve_kernel, out_shape=shape((8, 1, LANES)),
                          in_specs=vmem(1), out_specs=vmem(1)[0], name="solve")(parts)


def model_of(details, answers, images):
    block = 32
    return pl.pallas_call(
        model_kernel,
        out_shape=shape((4 * LANES, LANES), jnp.bfloat16),
        grid=(2 * LANES // block,),
        in_specs=[pl.BlockSpec(memory_space=pltpu.SMEM),
                  pl.BlockSpec((8, LANES), lambda g: (0, 0)),
                  pl.BlockSpec((block * ROWS, 2 * LANES), lambda g: (g, 0))],
        out_specs=pl.BlockSpec((2 * block, LANES), lambda g: (g, 0)),
        scratch_shapes=[pltpu.VMEM((VIS_DEV, ROWS, LANES), jnp.float32),
                        pltpu.VMEM((block * 16, LANES), jnp.float32)],
        compiler_params=params(), name="model",
    )(details, answers, images)


def final(slots, science, returned):
    return pl.pallas_call(final_kernel, out_shape=shape((2 * LANES, LANES)),
                          in_specs=vmem(3), out_specs=vmem(1)[0], name="final")(slots, science, returned)


def exchange(values, groups=None):
    return lax.all_to_all(values, "patch", split_axis=0, concat_axis=0, tiled=True,
                          axis_index_groups=groups)


def per_device(science, inverse_sigma, template, destination, offsets, visit_local):
    patches = lax.axis_size("patch")
    planes = [[z * 8 + i for i in range(8)] for z in range(patches // 8)]
    lines = [[z * 8 + i for z in range(patches // 8)] for i in range(8)]
    band, wide_p, wide_q = constants()
    whole_template = lax.all_gather(template[0].astype(jnp.bfloat16), "visit", axis=0, tiled=True)
    science_rows = science.reshape(2 * LANES, LANES)
    packed, slots = pack(science_rows, inverse_sigma.reshape(2 * LANES, LANES),
                         destination.reshape(1, LANES), visit_local.reshape(1, LANES), offsets.T)
    arrived = exchange(packed.reshape(patches, 5, 2, LANES)).reshape(LANES * SLOT_ROWS, LANES)
    images, gram, details = fit(arrived, whole_template, band, wide_p, wide_q)
    parts = exchange(gram.reshape(8, 16, LANES), planes)
    parts = exchange(middle(parts), lines)
    answers = exchange(solve(parts), planes).reshape(8, LANES)
    model = model_of(details, answers, images)
    returned = exchange(model.reshape(patches, 2, 2, LANES)).reshape(4 * LANES, LANES)
    difference = final(slots, science_rows, returned)
    table = jnp.concatenate([answers[:, 0:32], answers[:, 32:64]], axis=1).reshape(VIS_DEV, ROWS)
    coefficients = jnp.stack([table[:, k] for k in basis_rows()], axis=1)
    return difference.reshape(science.shape), coefficients


def solution(mesh):
    return jax.shard_map(
        per_device,
        mesh=mesh,
        in_specs=(
            P(("patch", "visit"), None, None),
            P(("patch", "visit"), None, None),
            P("patch", "visit", None),
            P(("patch", "visit")),
            P(("patch", "visit"), None),
            P(("patch", "visit")),
        ),
        out_specs=(P(("patch", "visit"), None, None), P("visit", None)),
        check_vma=False,
    )
```

```python
import functools

import jax
import jax.numpy as jnp
import numpy as np
from jax import lax
from jax.experimental import pallas as pl
from jax.experimental.pallas import tpu as pltpu
from jax.sharding import PartitionSpec as P

KR = 10
TAPS = 2 * KR + 1
NB = 28
VIS_DEV = 16
ROWS = 32
LANES = 128
GROUP = 16
DEPTH = 160
FILTER_ROWS = 80
FILTER_BAND = 656
FILTER_DEPTH = 112
SLOT_ROWS = 10

gauss_widths = (1.0, 2.0, 4.0)
poly_degrees = (4, 2, 2)

SET_P = (0, 1, 2, 3, 4, 5, 6, 7)
SET_Q = (8, 9, 10, 0, 1, 0, 8, 9)
COLS_P = (0, 1, 2, 5, 6, 7)
COLS_Q = (8, 3, 4, 9, 10)

ROW_PAIRS = (
    [(0, b) for b in range(5)] + [(5, 5), (5, 6), (5, 7)]
    + [(1, b) for b in range(4)] + [None, (6, 5), (6, 6), None]
    + [(2, 0), (2, 1), (2, 2), None, None, (7, 5), (10, 8), None]
    + [(8, 8), (8, 9), (8, 10), (3, 0), (3, 1), (4, 0), (9, 8), (9, 9)]
)
WEIGHT_ROW = 12
SCIENCE_ROW = 15


def filter_table(radius):
    tap_points = np.arange(-radius, radius + 1) * 1.0
    raw_columns = []
    for width_value, degree in zip(gauss_widths, poly_degrees):
        bell_curve = np.exp(-tap_points * tap_points / (2.0 * width_value * width_value))
        for power_index in range(degree + 1):
            raw_columns.append(bell_curve * (tap_points / radius) ** power_index)
    orthonormal = []
    for column in raw_columns:
        vector = column.copy()
        for repeat_index in range(2):
            for earlier in orthonormal:
                vector = vector - np.dot(earlier, vector) * earlier
        orthonormal.append(vector / np.sqrt(np.dot(vector, vector)))
    return np.stack(orthonormal, axis=1).astype(np.float32)


def basis_rows():
    rows = []
    offset = 0
    for degree in poly_degrees:
        for first in range(degree + 1):
            for second in range(degree + 1 - first):
                rows.append(ROW_PAIRS.index((offset + first, offset + second)))
        offset += degree + 1
    return rows + [WEIGHT_ROW]


def constants():
    values = filter_table(KR)
    band = np.zeros((2 * FILTER_BAND, FILTER_DEPTH), np.float32)
    for which, held in enumerate((SET_P, SET_Q)):
        for y in range(FILTER_ROWS + 1):
            for row, b in enumerate(held):
                band[which * FILTER_BAND + y * 8 + row, y : y + TAPS] = values[:, b]
    columns = []
    for held in (COLS_P, COLS_Q):
        wide = np.zeros((DEPTH, len(held) * LANES), np.float32)
        for place, a in enumerate(held):
            for j in range(LANES):
                wide[j : j + TAPS, place * LANES + j] = values[:, a]
        columns.append(wide)
    return [jnp.asarray(c).astype(jnp.bfloat16) for c in (band, *columns)]


def iota(shape, axis):
    return lax.broadcasted_iota(jnp.int32, shape, axis)


def pack_kernel(science, sigma, dest, visit, offsets, packed, slots, stack):
    d = jnp.broadcast_to(dest[...], (LANES, LANES))
    earlier = (d.T == d) & (iota(d.shape, 0) < iota(d.shape, 1))
    rank = jnp.sum(jnp.where(earlier, 1, 0), axis=0, keepdims=True)
    slots[...] = jnp.broadcast_to(dest[...] * 2 + rank, slots.shape)
    for i in range(2):
        weight = sigma[pl.ds(i, LANES, stride=2), :]
        scaled = science[pl.ds(i, LANES, stride=2), :] * weight
        stack[i * LANES : (i + 1) * LANES, :] = scaled.astype(jnp.bfloat16)
        stack[(2 + i) * LANES : (3 + i) * LANES, :] = weight.astype(jnp.bfloat16)
    column = offsets[1:2, :]
    fields = (visit[...], offsets[0:1, :], column >> 7, column & 127)
    row = iota((LANES, LANES), 0)
    details = jnp.zeros((LANES, LANES), jnp.float32)
    for place, field in enumerate(fields):
        details = jnp.where(row == place, field.astype(jnp.float32), details)
    stack[4 * LANES :, :] = details.T.astype(jnp.bfloat16)
    first = dest[...] * SLOT_ROWS
    targets = (first + 2 * rank, first + 2 * rank + 1, first + 4 + 2 * rank,
               first + 5 + 2 * rank, first + 8 + rank)
    target = jnp.concatenate(targets, axis=1)
    block = 256
    for start in range(0, packed.shape[0], block):
        chosen = iota((block, 5 * LANES), 0) + start == target
        chosen = jnp.where(chosen, 1.0, 0.0).astype(jnp.bfloat16)
        packed[start : start + block, :] = jnp.dot(
            chosen, stack[...], preferred_element_type=jnp.float32
        ).astype(jnp.bfloat16)


def fit_kernel(place, arrived, own, next_1, next_2, next_3, band, wide_p, wide_q,
               images, gram, details_out,
               template, rows, data, left_p, left_q, right_p, right_q, design,
               total, details, sem):
    data[...] = arrived[...].astype(jnp.float32)
    for c in range(2):
        fields = data[pl.ds(8 + c, LANES, stride=SLOT_ROWS), :].T[0:8, :].astype(jnp.int32)
        line = iota((8, LANES), 0)
        at = (fields[1:2, :] * 9 + fields[2:3, :]) * 2
        turn = (LANES - fields[3:4, :]) & 127
        fields = jnp.where(line == 1, at, jnp.where(line == 2, turn, fields))
        details_out[c] = fields
    copy = pltpu.make_async_copy(details_out, details, sem)
    copy.start()
    for m, part in enumerate((own, next_1, next_2, next_3)):
        at = pl.multiple_of((place[0] ^ m) * 64, 64)
        template[pl.ds(at, 64), :] = part[...]
    for y0 in range(0, 240, FILTER_ROWS):
        depth = min(FILTER_DEPTH, 256 - y0)
        made = jnp.dot(band[:, 0:depth], template[y0 : y0 + depth, :],
                       preferred_element_type=jnp.float32)
        for which in range(2):
            for y in range(FILTER_ROWS):
                if y0 + y < 236:
                    first = which * FILTER_BAND + y * 8
                    pair = made[first : first + 16, :].astype(jnp.bfloat16)
                    for tile in range(8):
                        rows[((y0 + y) * 9 + tile) * 2 + which] = pair[:, tile * LANES : (tile + 1) * LANES]
    empty = jnp.zeros((16, LANES), jnp.bfloat16)
    for y in range(236):
        for which in range(2):
            rows[(y * 9 + 8) * 2 + which] = empty
    total[...] = jnp.zeros_like(total)
    copy.wait()
    lane = iota((16, LANES), 1)
    sub = iota((8, LANES), 0)
    quarter = iota((ROWS, LANES), 1) >> 5
    groups = 2 * LANES // GROUP

    def gather(g, side):
        for t in range(GROUP):
            c = t % 2
            src = g * (GROUP // 2) + t // 2
            at = details[c, 1, src]
            back = details[c, 2, src]
            keep = lane < LANES - details[c, 3, src]
            for which, left in enumerate((left_p, left_q)):
                turned = [pltpu.roll(rows[at + 2 * m + which], back, 1) for m in range(3)]
                for m in range(2):
                    left[side, t * 16 : t * 16 + 16, m * LANES : (m + 1) * LANES] = jnp.where(
                        keep, turned[m], turned[m + 1]
                    )

    def filter_columns(side):
        right_p[side] = jnp.dot(left_p[side, :, 0:DEPTH], wide_p[...], preferred_element_type=jnp.float32)
        right_q[side] = jnp.dot(left_q[side, :, 0:DEPTH], wide_q[...], preferred_element_type=jnp.float32)

    def combine(g, side):
        for t in range(GROUP):
            c = t % 2
            src = g * (GROUP // 2) + t // 2
            for i in range(2):
                at = t * 16 + i * 8

                def p(a):
                    k = COLS_P.index(a)
                    return right_p[side, at : at + 8, k * LANES : (k + 1) * LANES]

                def q(a):
                    k = COLS_Q.index(a)
                    return right_q[side, at : at + 8, k * LANES : (k + 1) * LANES]

                v0 = jnp.where(sub < 5, p(0), p(5))
                v1 = jnp.where(sub < 4, p(1), jnp.where(sub == 7, 0.0, p(6)))
                v1 = jnp.where(sub == 4, 1.0, v1)
                v2 = jnp.where(sub < 3, p(2), jnp.where(sub == 5, p(7), jnp.where(sub == 6, q(10), 0.0)))
                v3 = jnp.where(sub < 3, q(8), jnp.where(sub < 5, q(3), jnp.where(sub < 6, q(4), q(9))))
                lanes = slice(i * LANES, (i + 1) * LANES)
                first = pl.multiple_of((g * GROUP + t) * ROWS, ROWS)
                for m, v in enumerate((v0, v1, v2, v3)):
                    images[pl.ds(first + 8 * m, 8), lanes] = v
                weight = data[pl.ds(src * SLOT_ROWS + 4 + 2 * c + i, 1), :]
                science = data[pl.ds(src * SLOT_ROWS + 2 * c + i, 1), :]
                d1 = jnp.where(sub == 7, science, v1 * weight)
                whole = jnp.concatenate([v0 * weight, d1, v2 * weight, v3 * weight], axis=0)
                design[side, t * ROWS : (t + 1) * ROWS, lanes] = whole.astype(jnp.bfloat16)

    def accumulate(g, side, valid):
        for h in range(GROUP // 4):
            part = design[side, h * 128 : (h + 1) * 128, :]
            product = lax.dot_general(part, part, (((1,), (1,)), ((), ())),
                                      preferred_element_type=jnp.float32)
            for n in range(4):
                t = h * 4 + n
                v = details[t % 2, 0, g * (GROUP // 2) + t // 2]
                mine = quarter == jnp.where(valid, n, -1)
                total[v] += jnp.where(mine, product[n * ROWS : (n + 1) * ROWS, :], 0.0)

    def step(j, carry):
        for side in range(2):
            g = 2 * j + side
            old = g - 2
            accumulate(jnp.clip(old, 0, groups - 1), side, (old >= 0) & (old < groups))
            combine(jnp.clip(g - 1, 0, groups - 1), 1 - side)
            filter_columns(side)
            gather(jnp.minimum(g + 1, groups - 1), 1 - side)
        return carry

    gather(0, 0)
    lax.fori_loop(0, (groups + 2) // 2, step, 0)
    lane8 = iota((8, LANES), 1) >> 5
    for v in range(VIS_DEV):
        whole = total[v]
        whole = whole + pltpu.roll(whole, 64, 1)
        whole = whole + pltpu.roll(whole, 32, 1)
        low = jnp.where(lane8 == 0, whole[0:8], whole[8:16])
        high = jnp.where(lane8 == 2, whole[16:24], whole[24:32])
        gram[v * 8 : v * 8 + 8, :] = jnp.where(lane8 < 2, low, high)


def middle_kernel(parts, out):
    whole = parts[0]
    for n in range(1, parts.shape[0]):
        whole = whole + parts[n]
    for n in range(out.shape[0]):
        out[n] = whole


def solve_kernel(parts, out):
    whole = parts[0]
    for n in range(1, parts.shape[0]):
        whole = whole + parts[n]
    lane8 = iota((8, LANES), 1) >> 5
    pieces = []
    for p in range(4):
        piece = jnp.zeros((8, LANES), jnp.float32)
        for h in range(2):
            turned = whole[h * 8 : h * 8 + 8]
            shift = (32 * h - 32 * p) % LANES
            if shift:
                turned = pltpu.roll(turned, shift, 1)
            piece = jnp.where(lane8 == h, turned, piece)
        pieces.append(piece)
    matrix = jnp.concatenate(pieces, axis=0)
    lane = iota((ROWS, LANES), 1)
    row_lane = iota((1, LANES), 1)
    half = lane < 32
    for k in basis_rows():
        row = matrix[k : k + 1, :]
        column = jnp.where(half, matrix[:, k : k + 1], matrix[:, 32 + k : 33 + k])
        pivot = jnp.broadcast_to(column[k : k + 1, :], (ROWS, LANES))
        scaled = column / pivot
        matrix = jnp.where((lane & 31) == k, scaled, matrix - scaled * row)
    answer = matrix[SCIENCE_ROW : SCIENCE_ROW + 1, :]
    valid = row_lane < 0
    for k in basis_rows():
        valid = valid | ((row_lane & 31) == k)
    answer = jnp.where(valid & (row_lane < 64), answer, 0.0)
    for n in range(out.shape[0]):
        out[n] = answer


def model_kernel(details, answers, images, model, wide, sums):
    turned = jnp.concatenate([answers[...], jnp.zeros((LANES - 8, LANES), jnp.float32)], axis=0).T
    for v in range(VIS_DEV):
        piece = turned[(v % 2) * ROWS : (v % 2) * ROWS + ROWS, v // 2 : v // 2 + 1]
        wide[v] = jnp.broadcast_to(piece, (ROWS, LANES))
    block = 16

    def step(g, carry):
        for t in range(block):
            v = details[t % 2, 0, g * (block // 2) + t // 2]
            scale = [wide[v, 8 * m : 8 * m + 8] for m in range(4)]
            first = pl.multiple_of((g * block + t) * ROWS, ROWS)
            for i in range(2):
                lanes = slice(i * LANES, (i + 1) * LANES)
                acc = scale[0] * images[pl.ds(first, 8), lanes]
                for m in range(1, 4):
                    acc = acc + scale[m] * images[pl.ds(first + 8 * m, 8), lanes]
                sums[(2 * t + i) * 8 : (2 * t + i) * 8 + 8, :] = acc
        out = sums[pl.ds(0, 2 * block, stride=8), :]
        for n in range(1, 8):
            out = out + sums[pl.ds(n, 2 * block, stride=8), :]
        model[pl.ds(pl.multiple_of(g * 2 * block, 2 * block), 2 * block), :] = out.astype(jnp.bfloat16)
        return carry

    lax.fori_loop(0, 2 * LANES // block, step, 0)


def order_kernel(answers, out):
    row, place = iota((LANES, NB), 0), iota((LANES, NB), 1)
    for h in range(2):
        chosen = row < 0
        for k, at in enumerate(basis_rows()):
            chosen = chosen | ((place == k) & (row == 32 * h + at))
        out[pl.ds(h, 8, stride=2), :] = jnp.dot(
            answers[...], jnp.where(chosen, 1.0, 0.0), precision=lax.Precision.HIGHEST,
            preferred_element_type=jnp.float32)


def final_kernel(slots, science, returned, out):
    column = jnp.broadcast_to(slots[0:1, :], (LANES, LANES)).T
    column = jnp.concatenate([column] * 4, axis=1)
    for i in range(2):
        chosen = iota((LANES, 4 * LANES), 1) == column * 2 + i
        chosen = jnp.where(chosen, 1.0, 0.0).astype(jnp.bfloat16)
        model = jnp.dot(chosen, returned[...], preferred_element_type=jnp.float32)
        out[pl.ds(i, LANES, stride=2), :] = science[pl.ds(i, LANES, stride=2), :] - model


def vmem(count):
    return [pl.BlockSpec(memory_space=pltpu.VMEM)] * count


def shape(dims, dtype=jnp.float32):
    return jax.ShapeDtypeStruct(dims, dtype)


def params(mebibytes):
    return pltpu.CompilerParams(vmem_limit_bytes=mebibytes << 20)


def pack(science, sigma, dest, visit, offsets):
    return pl.pallas_call(
        pack_kernel,
        out_shape=(shape((LANES * SLOT_ROWS, LANES), jnp.bfloat16), shape((8, LANES), jnp.int32)),
        in_specs=vmem(5), out_specs=tuple(vmem(2)),
        scratch_shapes=[pltpu.VMEM((5 * LANES, LANES), jnp.bfloat16)],
        compiler_params=params(8), name="pack",
    )(science, sigma, dest, visit, offsets)


def fit(place, arrived, parts, band, wide_p, wide_q):
    return pl.pallas_call(
        fit_kernel,
        out_shape=(shape((2 * LANES * ROWS, 2 * LANES)), shape((VIS_DEV * 8, LANES)),
                   shape((2, 8, LANES), jnp.int32)),
        in_specs=[pl.BlockSpec(memory_space=pltpu.SMEM)] + vmem(8), out_specs=tuple(vmem(3)),
        scratch_shapes=[
            pltpu.VMEM((256, 1024), jnp.bfloat16),
            pltpu.VMEM((236 * 9 * 2, 16, LANES), jnp.bfloat16),
            pltpu.VMEM((LANES * SLOT_ROWS, LANES), jnp.float32),
            pltpu.VMEM((2, GROUP * 16, 256), jnp.bfloat16), pltpu.VMEM((2, GROUP * 16, 256), jnp.bfloat16),
            pltpu.VMEM((2, GROUP * 16, len(COLS_P) * LANES), jnp.float32),
            pltpu.VMEM((2, GROUP * 16, len(COLS_Q) * LANES), jnp.float32),
            pltpu.VMEM((2, GROUP * ROWS, 256), jnp.bfloat16),
            pltpu.VMEM((VIS_DEV, ROWS, LANES), jnp.float32),
            pltpu.SMEM((2, 8, LANES), jnp.int32), pltpu.SemaphoreType.DMA,
        ],
        compiler_params=params(40), name="fit",
    )(place, arrived, *parts, band, wide_p, wide_q)


def middle(parts):
    return pl.pallas_call(middle_kernel, out_shape=shape((16,) + parts.shape[1:]),
                          in_specs=vmem(1), out_specs=vmem(1)[0], compiler_params=params(4), name="middle")(parts)


def solve(parts):
    return pl.pallas_call(solve_kernel, out_shape=shape((8, 1, LANES)),
                          in_specs=vmem(1), out_specs=vmem(1)[0], compiler_params=params(4), name="solve")(parts)


def model_of(details, answers, images):
    return pl.pallas_call(
        model_kernel,
        out_shape=shape((4 * LANES, LANES), jnp.bfloat16),
        in_specs=[pl.BlockSpec(memory_space=pltpu.SMEM)] + vmem(2),
        out_specs=vmem(1)[0],
        scratch_shapes=[pltpu.VMEM((VIS_DEV, ROWS, LANES), jnp.float32),
                        pltpu.VMEM((16 * 16, LANES), jnp.float32)],
        compiler_params=params(14), name="model",
    )(details, answers, images)


def order(answers):
    return pl.pallas_call(order_kernel, out_shape=shape((VIS_DEV, NB)), in_specs=vmem(1),
                          out_specs=vmem(1)[0], compiler_params=params(4), name="order")(answers)


def final(slots, science, returned):
    return pl.pallas_call(final_kernel, out_shape=shape((2 * LANES, LANES)),
                          in_specs=vmem(3), out_specs=vmem(1)[0], compiler_params=params(4), name="final")(slots, science, returned)


def exchange(values, groups=None):
    return lax.all_to_all(values, "patch", split_axis=0, concat_axis=0, tiled=True,
                          axis_index_groups=groups)


def per_device(science, inverse_sigma, template, destination, offsets, visit_local):
    patches = lax.axis_size("patch")
    planes = [[z * 8 + i for i in range(8)] for z in range(patches // 8)]
    lines = [[z * 8 + i for z in range(patches // 8)] for i in range(8)]
    band, wide_p, wide_q = constants()
    own = template[0].astype(jnp.bfloat16)
    parts = [own] + [lax.ppermute(own, "visit", [(x, x ^ m) for x in range(4)]) for m in (1, 2, 3)]
    place = lax.axis_index("visit").astype(jnp.int32).reshape(1)
    science_rows = science.reshape(2 * LANES, LANES)
    packed, slots = pack(science_rows, inverse_sigma.reshape(2 * LANES, LANES),
                         destination.reshape(1, LANES), visit_local.reshape(1, LANES), offsets.T)
    arrived = exchange(packed.reshape(patches, 5, 2, LANES)).reshape(LANES * SLOT_ROWS, LANES)
    images, gram, details = fit(place, arrived, parts, band, wide_p, wide_q)
    parts = exchange(gram.reshape(8, 16, LANES), planes)
    parts = exchange(middle(parts), lines)
    answers = exchange(solve(parts), planes).reshape(8, LANES)
    model = model_of(details, answers, images)
    returned = exchange(model.reshape(patches, 2, 2, LANES)).reshape(4 * LANES, LANES)
    difference = final(slots, science_rows, returned)
    coefficients = order(answers)
    return difference.reshape(science.shape), coefficients


def solution(mesh):
    return jax.shard_map(
        per_device,
        mesh=mesh,
        in_specs=(
            P(("patch", "visit"), None, None),
            P(("patch", "visit"), None, None),
            P("patch", "visit", None),
            P(("patch", "visit")),
            P(("patch", "visit"), None),
            P(("patch", "visit")),
        ),
        out_specs=(P(("patch", "visit"), None, None), P("visit", None)),
        check_vma=False,
    )
```

```python
import functools

import jax
import jax.numpy as jnp
import numpy as np
from jax import lax
from jax.experimental import pallas as pl
from jax.experimental.pallas import tpu as pltpu
from jax.sharding import PartitionSpec as P

KR = 10
TAPS = 2 * KR + 1
NB = 28
VIS_DEV = 16
ROWS = 32
LANES = 128
GROUP = 16
DEPTH = 160
FILTER_ROWS = 80
FILTER_BAND = 656
FILTER_DEPTH = 112
SLOT_ROWS = 10

gauss_widths = (1.0, 2.0, 4.0)
poly_degrees = (4, 2, 2)

SET_P = (0, 1, 2, 3, 4, 5, 6, 7)
SET_Q = (8, 9, 10, 0, 1, 0, 8, 9)
COLS_P = (0, 1, 2, 5, 6, 7)
COLS_Q = (8, 3, 4, 9, 10)

ROW_PAIRS = (
    [(0, b) for b in range(5)] + [(5, 5), (5, 6), (5, 7)]
    + [(1, b) for b in range(4)] + [None, (6, 5), (6, 6), None]
    + [(2, 0), (2, 1), (2, 2), None, None, (7, 5), (10, 8), None]
    + [(8, 8), (8, 9), (8, 10), (3, 0), (3, 1), (4, 0), (9, 8), (9, 9)]
)
WEIGHT_ROW = 12
SCIENCE_ROW = 15


def filter_table(radius):
    tap_points = np.arange(-radius, radius + 1) * 1.0
    raw_columns = []
    for width_value, degree in zip(gauss_widths, poly_degrees):
        bell_curve = np.exp(-tap_points * tap_points / (2.0 * width_value * width_value))
        for power_index in range(degree + 1):
            raw_columns.append(bell_curve * (tap_points / radius) ** power_index)
    orthonormal = []
    for column in raw_columns:
        vector = column.copy()
        for repeat_index in range(2):
            for earlier in orthonormal:
                vector = vector - np.dot(earlier, vector) * earlier
        orthonormal.append(vector / np.sqrt(np.dot(vector, vector)))
    return np.stack(orthonormal, axis=1).astype(np.float32)


def basis_rows():
    rows = []
    offset = 0
    for degree in poly_degrees:
        for first in range(degree + 1):
            for second in range(degree + 1 - first):
                rows.append(ROW_PAIRS.index((offset + first, offset + second)))
        offset += degree + 1
    return rows + [WEIGHT_ROW]


def constants():
    values = filter_table(KR)
    band = np.zeros((2 * FILTER_BAND, FILTER_DEPTH), np.float32)
    for which, held in enumerate((SET_P, SET_Q)):
        for y in range(FILTER_ROWS + 1):
            for row, b in enumerate(held):
                band[which * FILTER_BAND + y * 8 + row, y : y + TAPS] = values[:, b]
    columns = []
    for held in (COLS_P, COLS_Q):
        wide = np.zeros((DEPTH, len(held) * LANES), np.float32)
        for place, a in enumerate(held):
            for j in range(LANES):
                wide[j : j + TAPS, place * LANES + j] = values[:, a]
        columns.append(wide)
    return [jnp.asarray(c).astype(jnp.bfloat16) for c in (band, *columns)]


def iota(shape, axis):
    return lax.broadcasted_iota(jnp.int32, shape, axis)


def pack_kernel(science, sigma, dest, visit, offsets, packed, slots, stack):
    d = jnp.broadcast_to(dest[...], (LANES, LANES))
    earlier = (d.T == d) & (iota(d.shape, 0) < iota(d.shape, 1))
    rank = jnp.sum(jnp.where(earlier, 1, 0), axis=0, keepdims=True)
    slots[...] = jnp.broadcast_to(dest[...] * 2 + rank, slots.shape)
    for i in range(2):
        weight = sigma[pl.ds(i, LANES, stride=2), :]
        scaled = science[pl.ds(i, LANES, stride=2), :] * weight
        stack[i * LANES : (i + 1) * LANES, :] = scaled.astype(jnp.bfloat16)
        stack[(2 + i) * LANES : (3 + i) * LANES, :] = weight.astype(jnp.bfloat16)
    column = offsets[1:2, :]
    fields = (visit[...], offsets[0:1, :], column >> 7, column & 127)
    row = iota((LANES, LANES), 0)
    details = jnp.zeros((LANES, LANES), jnp.float32)
    for place, field in enumerate(fields):
        details = jnp.where(row == place, field.astype(jnp.float32), details)
    stack[4 * LANES :, :] = details.T.astype(jnp.bfloat16)
    first = dest[...] * SLOT_ROWS
    targets = (first + 2 * rank, first + 2 * rank + 1, first + 4 + 2 * rank,
               first + 5 + 2 * rank, first + 8 + rank)
    target = jnp.concatenate(targets, axis=1)
    block = 256
    for start in range(0, packed.shape[0], block):
        chosen = iota((block, 5 * LANES), 0) + start == target
        chosen = jnp.where(chosen, 1.0, 0.0).astype(jnp.bfloat16)
        packed[start : start + block, :] = jnp.dot(
            chosen, stack[...], preferred_element_type=jnp.float32
        ).astype(jnp.bfloat16)


def keep_kernel(place, own, next_1, next_2, next_3, band, wide_p, wide_q,
                template, kept_band, kept_p, kept_q):
    for m, part in enumerate((own, next_1, next_2, next_3)):
        at = pl.multiple_of((place[0] ^ m) * 64, 64)
        template[pl.ds(at, 64), :] = part[...]
    kept_band[...] = band[...]
    kept_p[...] = wide_p[...]
    kept_q[...] = wide_q[...]


def fit_kernel(arrived, template, band, wide_p, wide_q, images, gram, details_out,
               rows, data, left_p, left_q, right_p, right_q, design,
               total, details, sem):
    data[...] = arrived[...].astype(jnp.float32)
    for c in range(2):
        fields = data[pl.ds(8 + c, LANES, stride=SLOT_ROWS), :].T[0:8, :].astype(jnp.int32)
        line = iota((8, LANES), 0)
        at = (fields[1:2, :] * 9 + fields[2:3, :]) * 2
        turn = (LANES - fields[3:4, :]) & 127
        fields = jnp.where(line == 1, at, jnp.where(line == 2, turn, fields))
        details_out[c] = fields
    copy = pltpu.make_async_copy(details_out, details, sem)
    copy.start()
    for y0 in range(0, 240, FILTER_ROWS):
        depth = min(FILTER_DEPTH, 256 - y0)
        made = jnp.dot(band[:, 0:depth], template[y0 : y0 + depth, :],
                       preferred_element_type=jnp.float32)
        for which in range(2):
            for y in range(FILTER_ROWS):
                if y0 + y < 236:
                    first = which * FILTER_BAND + y * 8
                    pair = made[first : first + 16, :].astype(jnp.bfloat16)
                    for tile in range(8):
                        rows[((y0 + y) * 9 + tile) * 2 + which] = pair[:, tile * LANES : (tile + 1) * LANES]
    empty = jnp.zeros((16, LANES), jnp.bfloat16)
    for y in range(236):
        for which in range(2):
            rows[(y * 9 + 8) * 2 + which] = empty
    total[...] = jnp.zeros_like(total)
    copy.wait()
    lane = iota((16, LANES), 1)
    sub = iota((8, LANES), 0)
    quarter = iota((ROWS, LANES), 1) >> 5
    groups = 2 * LANES // GROUP

    def gather(g, side):
        for t in range(GROUP):
            c = t % 2
            src = g * (GROUP // 2) + t // 2
            at = details[c, 1, src]
            back = details[c, 2, src]
            keep = lane < LANES - details[c, 3, src]
            for which, left in enumerate((left_p, left_q)):
                turned = [pltpu.roll(rows[at + 2 * m + which], back, 1) for m in range(3)]
                for m in range(2):
                    left[side, t * 16 : t * 16 + 16, m * LANES : (m + 1) * LANES] = jnp.where(
                        keep, turned[m], turned[m + 1]
                    )

    def filter_columns(side):
        right_p[side] = jnp.dot(left_p[side, :, 0:DEPTH], wide_p[...], preferred_element_type=jnp.float32)
        right_q[side] = jnp.dot(left_q[side, :, 0:DEPTH], wide_q[...], preferred_element_type=jnp.float32)

    def combine(g, side):
        for t in range(GROUP):
            c = t % 2
            src = g * (GROUP // 2) + t // 2
            for i in range(2):
                at = t * 16 + i * 8

                def p(a):
                    k = COLS_P.index(a)
                    return right_p[side, at : at + 8, k * LANES : (k + 1) * LANES]

                def q(a):
                    k = COLS_Q.index(a)
                    return right_q[side, at : at + 8, k * LANES : (k + 1) * LANES]

                v0 = jnp.where(sub < 5, p(0), p(5))
                v1 = jnp.where(sub < 4, p(1), jnp.where(sub == 7, 0.0, p(6)))
                v1 = jnp.where(sub == 4, 1.0, v1)
                v2 = jnp.where(sub < 3, p(2), jnp.where(sub == 5, p(7), jnp.where(sub == 6, q(10), 0.0)))
                v3 = jnp.where(sub < 3, q(8), jnp.where(sub < 5, q(3), jnp.where(sub < 6, q(4), q(9))))
                lanes = slice(i * LANES, (i + 1) * LANES)
                first = pl.multiple_of((g * GROUP + t) * ROWS, ROWS)
                for m, v in enumerate((v0, v1, v2, v3)):
                    images[pl.ds(first + 8 * m, 8), lanes] = v
                weight = data[pl.ds(src * SLOT_ROWS + 4 + 2 * c + i, 1), :]
                science = data[pl.ds(src * SLOT_ROWS + 2 * c + i, 1), :]
                d1 = jnp.where(sub == 7, science, v1 * weight)
                whole = jnp.concatenate([v0 * weight, d1, v2 * weight, v3 * weight], axis=0)
                design[side, t * ROWS : (t + 1) * ROWS, lanes] = whole.astype(jnp.bfloat16)

    def accumulate(g, side):
        for h in range(GROUP // 4):
            part = design[side, h * 128 : (h + 1) * 128, :]
            product = lax.dot_general(part, part, (((1,), (1,)), ((), ())),
                                      preferred_element_type=jnp.float32)
            for n in range(4):
                t = h * 4 + n
                v = details[t % 2, 0, g * (GROUP // 2) + t // 2]
                total[v] += jnp.where(quarter == n, product[n * ROWS : (n + 1) * ROWS, :], 0.0)

    def step(j, carry):
        for side in range(2):
            g = 2 * j + side
            accumulate(g - 2, side)
            combine(g - 1, 1 - side)
            filter_columns(side)
            gather(jnp.minimum(g + 1, groups - 1), 1 - side)
        return carry

    gather(0, 0)
    filter_columns(0)
    gather(1, 1)
    combine(0, 0)
    filter_columns(1)
    gather(2, 0)
    lax.fori_loop(1, groups // 2, step, 0)
    accumulate(groups - 2, 0)
    combine(groups - 1, 1)
    accumulate(groups - 1, 1)
    lane8 = iota((8, LANES), 1) >> 5
    for v in range(VIS_DEV):
        whole = total[v]
        whole = whole + pltpu.roll(whole, 64, 1)
        whole = whole + pltpu.roll(whole, 32, 1)
        low = jnp.where(lane8 == 0, whole[0:8], whole[8:16])
        high = jnp.where(lane8 == 2, whole[16:24], whole[24:32])
        gram[v * 8 : v * 8 + 8, :] = jnp.where(lane8 < 2, low, high)


def middle_kernel(parts, out):
    whole = parts[0]
    for n in range(1, parts.shape[0]):
        whole = whole + parts[n]
    for n in range(out.shape[0]):
        out[n] = whole


def solve_kernel(parts, out):
    whole = parts[0]
    for n in range(1, parts.shape[0]):
        whole = whole + parts[n]
    lane8 = iota((8, LANES), 1) >> 5
    pieces = []
    for p in range(4):
        piece = jnp.zeros((8, LANES), jnp.float32)
        for h in range(2):
            turned = whole[h * 8 : h * 8 + 8]
            shift = (32 * h - 32 * p) % LANES
            if shift:
                turned = pltpu.roll(turned, shift, 1)
            piece = jnp.where(lane8 == h, turned, piece)
        pieces.append(piece)
    matrix = jnp.concatenate(pieces, axis=0)
    lane = iota((ROWS, LANES), 1)
    row_lane = iota((1, LANES), 1)
    half = lane < 32
    for k in basis_rows():
        row = matrix[k : k + 1, :]
        column = jnp.where(half, matrix[:, k : k + 1], matrix[:, 32 + k : 33 + k])
        pivot = jnp.broadcast_to(column[k : k + 1, :], (ROWS, LANES))
        scaled = column / pivot
        matrix = jnp.where((lane & 31) == k, scaled, matrix - scaled * row)
    answer = matrix[SCIENCE_ROW : SCIENCE_ROW + 1, :]
    valid = row_lane < 0
    for k in basis_rows():
        valid = valid | ((row_lane & 31) == k)
    answer = jnp.where(valid & (row_lane < 64), answer, 0.0)
    for n in range(out.shape[0]):
        out[n] = answer


def model_kernel(details, answers, images, model, wide, sums):
    turned = jnp.concatenate([answers[...], jnp.zeros((LANES - 8, LANES), jnp.float32)], axis=0).T
    for v in range(VIS_DEV):
        piece = turned[(v % 2) * ROWS : (v % 2) * ROWS + ROWS, v // 2 : v // 2 + 1]
        wide[v] = jnp.broadcast_to(piece, (ROWS, LANES))
    block = 16

    def step(g, carry):
        near = images.at[pl.ds(pl.multiple_of(g * block * ROWS, block * ROWS), block * ROWS), :]
        for t in range(block):
            v = details[t % 2, 0, g * (block // 2) + t // 2]
            scale = [wide[v, 8 * m : 8 * m + 8] for m in range(4)]
            first = t * ROWS
            for i in range(2):
                lanes = slice(i * LANES, (i + 1) * LANES)
                acc = scale[0] * near[first : first + 8, lanes]
                for m in range(1, 4):
                    acc = acc + scale[m] * near[first + 8 * m : first + 8 * m + 8, lanes]
                sums[(2 * t + i) * 8 : (2 * t + i) * 8 + 8, :] = acc
        out = sums[pl.ds(0, 2 * block, stride=8), :]
        for n in range(1, 8):
            out = out + sums[pl.ds(n, 2 * block, stride=8), :]
        model[pl.ds(pl.multiple_of(g * 2 * block, 2 * block), 2 * block), :] = out.astype(jnp.bfloat16)
        return carry

    lax.fori_loop(0, 2 * LANES // block, step, 0)


def order_kernel(answers, out):
    row, place = iota((LANES, NB), 0), iota((LANES, NB), 1)
    for h in range(2):
        chosen = row < 0
        for k, at in enumerate(basis_rows()):
            chosen = chosen | ((place == k) & (row == 32 * h + at))
        out[pl.ds(h, 8, stride=2), :] = jnp.dot(
            answers[...], jnp.where(chosen, 1.0, 0.0), precision=lax.Precision.HIGHEST,
            preferred_element_type=jnp.float32)


def final_kernel(slots, science, returned, out):
    column = jnp.broadcast_to(slots[0:1, :], (LANES, LANES)).T
    column = jnp.concatenate([column] * 4, axis=1)
    for i in range(2):
        chosen = iota((LANES, 4 * LANES), 1) == column * 2 + i
        chosen = jnp.where(chosen, 1.0, 0.0).astype(jnp.bfloat16)
        model = jnp.dot(chosen, returned[...], preferred_element_type=jnp.float32)
        out[pl.ds(i, LANES, stride=2), :] = science[pl.ds(i, LANES, stride=2), :] - model


def vmem(count):
    return [pl.BlockSpec(memory_space=pltpu.VMEM)] * count


def shape(dims, dtype=jnp.float32):
    return jax.ShapeDtypeStruct(dims, dtype)


def params(mebibytes):
    return pltpu.CompilerParams(vmem_limit_bytes=mebibytes << 20)


def pack(science, sigma, dest, visit, offsets):
    return pl.pallas_call(
        pack_kernel,
        out_shape=(shape((LANES * SLOT_ROWS, LANES), jnp.bfloat16), shape((8, LANES), jnp.int32)),
        in_specs=vmem(5), out_specs=tuple(vmem(2)),
        scratch_shapes=[pltpu.VMEM((5 * LANES, LANES), jnp.bfloat16)],
        compiler_params=params(60), name="pack",
    )(science, sigma, dest, visit, offsets)


def keep(place, parts, tables):
    return pl.pallas_call(
        keep_kernel,
        out_shape=(shape((256, 1024), jnp.bfloat16),) + tuple(shape(t.shape, t.dtype) for t in tables),
        in_specs=[pl.BlockSpec(memory_space=pltpu.SMEM)] + vmem(7), out_specs=tuple(vmem(4)),
        compiler_params=params(8), name="keep",
    )(place, *parts, *tables)


def fit(arrived, template, band, wide_p, wide_q):
    return pl.pallas_call(
        fit_kernel,
        out_shape=(shape((2 * LANES * ROWS, 2 * LANES)), shape((VIS_DEV * 8, LANES)),
                   shape((2, 8, LANES), jnp.int32)),
        in_specs=vmem(5), out_specs=tuple(vmem(3)),
        scratch_shapes=[
            pltpu.VMEM((236 * 9 * 2, 16, LANES), jnp.bfloat16),
            pltpu.VMEM((LANES * SLOT_ROWS, LANES), jnp.float32),
            pltpu.VMEM((2, GROUP * 16, 256), jnp.bfloat16), pltpu.VMEM((2, GROUP * 16, 256), jnp.bfloat16),
            pltpu.VMEM((2, GROUP * 16, len(COLS_P) * LANES), jnp.float32),
            pltpu.VMEM((2, GROUP * 16, len(COLS_Q) * LANES), jnp.float32),
            pltpu.VMEM((2, GROUP * ROWS, 256), jnp.bfloat16),
            pltpu.VMEM((VIS_DEV, ROWS, LANES), jnp.float32),
            pltpu.SMEM((2, 8, LANES), jnp.int32), pltpu.SemaphoreType.DMA,
        ],
        compiler_params=params(40), name="fit",
    )(arrived, template, band, wide_p, wide_q)


def middle(parts):
    return pl.pallas_call(middle_kernel, out_shape=shape((16,) + parts.shape[1:]),
                          in_specs=vmem(1), out_specs=vmem(1)[0], compiler_params=params(4), name="middle")(parts)


def solve(parts):
    return pl.pallas_call(solve_kernel, out_shape=shape((8, 1, LANES)),
                          in_specs=vmem(1), out_specs=vmem(1)[0], compiler_params=params(4), name="solve")(parts)


def model_of(details, answers, images):
    return pl.pallas_call(
        model_kernel,
        out_shape=shape((4 * LANES, LANES), jnp.bfloat16),
        in_specs=[pl.BlockSpec(memory_space=pltpu.SMEM)] + vmem(2),
        out_specs=vmem(1)[0],
        scratch_shapes=[pltpu.VMEM((VIS_DEV, ROWS, LANES), jnp.float32),
                        pltpu.VMEM((16 * 16, LANES), jnp.float32)],
        compiler_params=params(14), name="model",
    )(details, answers, images)


def order(answers):
    return pl.pallas_call(order_kernel, out_shape=shape((VIS_DEV, NB)), in_specs=vmem(1),
                          out_specs=vmem(1)[0], compiler_params=params(4), name="order")(answers)


def final(slots, science, returned):
    return pl.pallas_call(final_kernel, out_shape=shape((2 * LANES, LANES)),
                          in_specs=vmem(3), out_specs=vmem(1)[0], compiler_params=params(4), name="final")(slots, science, returned)


def exchange(values, groups=None):
    return lax.all_to_all(values, "patch", split_axis=0, concat_axis=0, tiled=True,
                          axis_index_groups=groups)


def per_device(science, inverse_sigma, template, destination, offsets, visit_local):
    patches = lax.axis_size("patch")
    planes = [[z * 8 + i for i in range(8)] for z in range(patches // 8)]
    lines = [[z * 8 + i for z in range(patches // 8)] for i in range(8)]
    own = template[0].astype(jnp.bfloat16)
    parts = [own] + [lax.ppermute(own, "visit", [(x, x ^ m) for x in range(4)]) for m in (1, 2, 3)]
    place = lax.axis_index("visit").astype(jnp.int32).reshape(1)
    science_rows = science.reshape(2 * LANES, LANES)
    packed, slots = pack(science_rows, inverse_sigma.reshape(2 * LANES, LANES),
                         destination.reshape(1, LANES), visit_local.reshape(1, LANES), offsets.T)
    kept = keep(place, parts, constants())
    arrived = exchange(packed.reshape(patches, 5, 2, LANES)).reshape(LANES * SLOT_ROWS, LANES)
    images, gram, details = fit(arrived, *kept)
    parts = exchange(gram.reshape(8, 16, LANES), planes)
    parts = exchange(middle(parts), lines)
    answers = exchange(solve(parts), planes).reshape(8, LANES)
    model = model_of(details, answers, images)
    returned = exchange(model.reshape(patches, 2, 2, LANES)).reshape(4 * LANES, LANES)
    difference = final(slots, science_rows, returned)
    coefficients = order(answers)
    return difference.reshape(science.shape), coefficients


def solution(mesh):
    return jax.shard_map(
        per_device,
        mesh=mesh,
        in_specs=(
            P(("patch", "visit"), None, None),
            P(("patch", "visit"), None, None),
            P("patch", "visit", None),
            P(("patch", "visit")),
            P(("patch", "visit"), None),
            P(("patch", "visit")),
        ),
        out_specs=(P(("patch", "visit"), None, None), P("visit", None)),
        check_vma=False,
    )
```

```python
import functools

import jax
import jax.numpy as jnp
import numpy as np
from jax import lax
from jax.experimental import pallas as pl
from jax.experimental.pallas import tpu as pltpu
from jax.sharding import PartitionSpec as P

KR = 10
TAPS = 2 * KR + 1
NB = 28
VIS_DEV = 16
ROWS = 32
LANES = 128
GROUP = 16
DEPTH = 160
SOLVE_BLOCK = 7
FILTER_ROWS = 80
FILTER_BAND = 656
FILTER_DEPTH = 112
SLOT_ROWS = 10

gauss_widths = (1.0, 2.0, 4.0)
poly_degrees = (4, 2, 2)

SET_P = (0, 1, 2, 3, 4, 5, 6, 7)
SET_Q = (8, 9, 10, 0, 1, 0, 8, 9)
COLS_P = (0, 1, 2, 5, 6, 7)
COLS_Q = (8, 3, 4, 9, 10)

ROW_PAIRS = (
    [(0, b) for b in range(5)] + [(5, 5), (5, 6), (5, 7)]
    + [(1, b) for b in range(4)] + [None, (6, 5), (6, 6), None]
    + [(2, 0), (2, 1), (2, 2), None, None, (7, 5), (10, 8), None]
    + [(8, 8), (8, 9), (8, 10), (3, 0), (3, 1), (4, 0), (9, 8), (9, 9)]
)
WEIGHT_ROW = 12
SCIENCE_ROW = 15


def filter_table(radius):
    tap_points = np.arange(-radius, radius + 1) * 1.0
    raw_columns = []
    for width_value, degree in zip(gauss_widths, poly_degrees):
        bell_curve = np.exp(-tap_points * tap_points / (2.0 * width_value * width_value))
        for power_index in range(degree + 1):
            raw_columns.append(bell_curve * (tap_points / radius) ** power_index)
    orthonormal = []
    for column in raw_columns:
        vector = column.copy()
        for repeat_index in range(2):
            for earlier in orthonormal:
                vector = vector - np.dot(earlier, vector) * earlier
        orthonormal.append(vector / np.sqrt(np.dot(vector, vector)))
    return np.stack(orthonormal, axis=1).astype(np.float32)


def basis_rows():
    rows = []
    offset = 0
    for degree in poly_degrees:
        for first in range(degree + 1):
            for second in range(degree + 1 - first):
                rows.append(ROW_PAIRS.index((offset + first, offset + second)))
        offset += degree + 1
    return rows + [WEIGHT_ROW]


def constants():
    values = filter_table(KR)
    band = np.zeros((2 * FILTER_BAND, FILTER_DEPTH), np.float32)
    for which, held in enumerate((SET_P, SET_Q)):
        for y in range(FILTER_ROWS + 1):
            for row, b in enumerate(held):
                band[which * FILTER_BAND + y * 8 + row, y : y + TAPS] = values[:, b]
    columns = []
    for held in (COLS_P, COLS_Q):
        wide = np.zeros((DEPTH, len(held) * LANES), np.float32)
        for place, a in enumerate(held):
            for j in range(LANES):
                wide[j : j + TAPS, place * LANES + j] = values[:, a]
        columns.append(wide)
    return [jnp.asarray(c).astype(jnp.bfloat16) for c in (band, *columns)]


def iota(shape, axis):
    return lax.broadcasted_iota(jnp.int32, shape, axis)


def pack_kernel(science, sigma, dest, visit, offsets, packed, slots, stack):
    d = jnp.broadcast_to(dest[...], (LANES, LANES))
    earlier = (d.T == d) & (iota(d.shape, 0) < iota(d.shape, 1))
    rank = jnp.sum(jnp.where(earlier, 1, 0), axis=0, keepdims=True)
    slots[...] = jnp.broadcast_to(dest[...] * 2 + rank, slots.shape)
    for i in range(2):
        weight = sigma[pl.ds(i, LANES, stride=2), :]
        scaled = science[pl.ds(i, LANES, stride=2), :] * weight
        stack[i * LANES : (i + 1) * LANES, :] = scaled.astype(jnp.bfloat16)
        stack[(2 + i) * LANES : (3 + i) * LANES, :] = weight.astype(jnp.bfloat16)
    column = offsets[1:2, :]
    fields = (visit[...], offsets[0:1, :], column >> 7, column & 127)
    row = iota((LANES, LANES), 0)
    details = jnp.zeros((LANES, LANES), jnp.float32)
    for place, field in enumerate(fields):
        details = jnp.where(row == place, field.astype(jnp.float32), details)
    stack[4 * LANES :, :] = details.T.astype(jnp.bfloat16)
    first = dest[...] * SLOT_ROWS
    targets = (first + 2 * rank, first + 2 * rank + 1, first + 4 + 2 * rank,
               first + 5 + 2 * rank, first + 8 + rank)
    target = jnp.concatenate(targets, axis=1)
    block = 256
    for start in range(0, packed.shape[0], block):
        chosen = iota((block, 5 * LANES), 0) + start == target
        chosen = jnp.where(chosen, 1.0, 0.0).astype(jnp.bfloat16)
        packed[start : start + block, :] = jnp.dot(
            chosen, stack[...], preferred_element_type=jnp.float32
        ).astype(jnp.bfloat16)


def keep_kernel(place, own, next_1, next_2, next_3, band, wide_p, wide_q,
                template, kept_band, kept_p, kept_q):
    for m, part in enumerate((own, next_1, next_2, next_3)):
        at = pl.multiple_of((place[0] ^ m) * 64, 64)
        template[pl.ds(at, 64), :] = part[...]
    kept_band[...] = band[...]
    kept_p[...] = wide_p[...]
    kept_q[...] = wide_q[...]


def fit_kernel(arrived, template, band, wide_p, wide_q, images, gram, details_out,
               rows, data, left_p, left_q, right_p, right_q, design,
               total, details, sem):
    data[...] = arrived[...].astype(jnp.float32)
    for c in range(2):
        fields = data[pl.ds(8 + c, LANES, stride=SLOT_ROWS), :].T[0:8, :].astype(jnp.int32)
        line = iota((8, LANES), 0)
        at = (fields[1:2, :] * 9 + fields[2:3, :]) * 2
        turn = (LANES - fields[3:4, :]) & 127
        fields = jnp.where(line == 1, at, jnp.where(line == 2, turn, fields))
        details_out[c] = fields
    copy = pltpu.make_async_copy(details_out, details, sem)
    copy.start()
    for y0 in range(0, 240, FILTER_ROWS):
        depth = min(FILTER_DEPTH, 256 - y0)
        made = jnp.dot(band[:, 0:depth], template[y0 : y0 + depth, :],
                       preferred_element_type=jnp.float32)
        for which in range(2):
            for y in range(FILTER_ROWS):
                if y0 + y < 236:
                    first = which * FILTER_BAND + y * 8
                    pair = made[first : first + 16, :].astype(jnp.bfloat16)
                    for tile in range(8):
                        rows[((y0 + y) * 9 + tile) * 2 + which] = pair[:, tile * LANES : (tile + 1) * LANES]
    empty = jnp.zeros((16, LANES), jnp.bfloat16)
    for y in range(236):
        for which in range(2):
            rows[(y * 9 + 8) * 2 + which] = empty
    total[...] = jnp.zeros_like(total)
    copy.wait()
    lane = iota((16, LANES), 1)
    sub = iota((8, LANES), 0)
    quarter = iota((ROWS, LANES), 1) >> 5
    groups = 2 * LANES // GROUP

    def gather(g, side):
        for t in range(GROUP):
            c = t % 2
            src = g * (GROUP // 2) + t // 2
            at = details[c, 1, src]
            back = details[c, 2, src]
            keep = lane < LANES - details[c, 3, src]
            for which, left in enumerate((left_p, left_q)):
                turned = [pltpu.roll(rows[at + 2 * m + which], back, 1) for m in range(3)]
                for m in range(2):
                    left[side, t * 16 : t * 16 + 16, m * LANES : (m + 1) * LANES] = jnp.where(
                        keep, turned[m], turned[m + 1]
                    )

    def filter_columns(side):
        right_p[side] = jnp.dot(left_p[side, :, 0:DEPTH], wide_p[...], preferred_element_type=jnp.float32)
        right_q[side] = jnp.dot(left_q[side, :, 0:DEPTH], wide_q[...], preferred_element_type=jnp.float32)

    def combine(g, side):
        for t in range(GROUP):
            c = t % 2
            src = g * (GROUP // 2) + t // 2
            for i in range(2):
                at = t * 16 + i * 8

                def p(a):
                    k = COLS_P.index(a)
                    return right_p[side, at : at + 8, k * LANES : (k + 1) * LANES]

                def q(a):
                    k = COLS_Q.index(a)
                    return right_q[side, at : at + 8, k * LANES : (k + 1) * LANES]

                v0 = jnp.where(sub < 5, p(0), p(5))
                v1 = jnp.where(sub < 4, p(1), jnp.where(sub == 7, 0.0, p(6)))
                v1 = jnp.where(sub == 4, 1.0, v1)
                v2 = jnp.where(sub < 3, p(2), jnp.where(sub == 5, p(7), jnp.where(sub == 6, q(10), 0.0)))
                v3 = jnp.where(sub < 3, q(8), jnp.where(sub < 5, q(3), jnp.where(sub < 6, q(4), q(9))))
                lanes = slice(i * LANES, (i + 1) * LANES)
                first = pl.multiple_of((g * GROUP + t) * ROWS, ROWS)
                for m, v in enumerate((v0, v1, v2, v3)):
                    images[pl.ds(first + 8 * m, 8), lanes] = v
                weight = data[pl.ds(src * SLOT_ROWS + 4 + 2 * c + i, 1), :]
                science = data[pl.ds(src * SLOT_ROWS + 2 * c + i, 1), :]
                d1 = jnp.where(sub == 7, science, v1 * weight)
                whole = jnp.concatenate([v0 * weight, d1, v2 * weight, v3 * weight], axis=0)
                design[side, t * ROWS : (t + 1) * ROWS, lanes] = whole.astype(jnp.bfloat16)

    def accumulate(g, side):
        for h in range(GROUP // 4):
            part = design[side, h * 128 : (h + 1) * 128, :]
            product = lax.dot_general(part, part, (((1,), (1,)), ((), ())),
                                      preferred_element_type=jnp.float32)
            for n in range(4):
                t = h * 4 + n
                v = details[t % 2, 0, g * (GROUP // 2) + t // 2]
                total[v] += jnp.where(quarter == n, product[n * ROWS : (n + 1) * ROWS, :], 0.0)

    def step(j, carry):
        for side in range(2):
            g = 2 * j + side
            accumulate(g - 2, side)
            combine(g - 1, 1 - side)
            filter_columns(side)
            gather(jnp.minimum(g + 1, groups - 1), 1 - side)
        return carry

    gather(0, 0)
    filter_columns(0)
    gather(1, 1)
    combine(0, 0)
    filter_columns(1)
    gather(2, 0)
    lax.fori_loop(1, groups // 2, step, 0)
    accumulate(groups - 2, 0)
    combine(groups - 1, 1)
    accumulate(groups - 1, 1)
    lane8 = iota((8, LANES), 1)
    line = lane8[0:2] >> 5
    for c in range(VIS_DEV // 2):
        sums = []
        for v in (2 * c, 2 * c + 1):
            whole = total[v]
            whole = whole + pltpu.roll(whole, 64, 1)
            sums.append(whole + pltpu.roll(whole, 32, 1))
        first, second = ([w[8 * p : 8 * p + 8] for p in range(4)] for w in sums)
        upper = [jnp.where(lane8 < 64, x, y) for x, y in zip(first, second)]
        place = lane8 & 63
        main = jnp.where(place < 32, upper[0], upper[1])
        gram[10 * c : 10 * c + 8, :] = jnp.where(
            (place >= 32) & (place < 40),
            jnp.where(lane8 < 64, pltpu.roll(first[3], 8, 1), pltpu.roll(second[3], 8, 1)), main)
        extra = jnp.where((lane8 & 31) < 16, pltpu.roll(first[2], 16, 1), second[2])
        low = jnp.where(line == 0, extra[0:2], extra[2:4])
        high = jnp.where(line == 2, extra[4:6], extra[6:8])
        gram[10 * c + 8 : 10 * c + 10, :] = jnp.where(line < 2, low, high)


def total_of(parts):
    main, extra = parts[0:8, :], parts[8:10, :]
    for n in range(10, parts.shape[0], 10):
        main = main + parts[n : n + 8, :]
        extra = extra + parts[n + 8 : n + 10, :]
    return main, extra


def middle_kernel(parts, out):
    main, extra = total_of(parts)
    for n in range(0, out.shape[0], 10):
        out[n : n + 8, :] = main
        out[n + 8 : n + 10, :] = extra


def solve_kernel(parts, out):
    main, extra = total_of(parts)
    rest = jnp.concatenate([extra if m == 0 else pltpu.roll(extra, 128 - 32 * m, 1) for m in range(4)], axis=0)
    lane8 = iota((8, LANES), 1)
    turns = ((main, 0, 96), (main, 96, 64), (rest, 16, 32), (main, 120, 88))
    pieces = []
    for p, (source, near, far) in enumerate(turns):
        near = pltpu.roll(source, near, 1) if near else source
        piece = jnp.where(lane8 < 32, near, pltpu.roll(source, far, 1))
        pieces.append(jnp.where((lane8 < 64) & ((lane8 & 31) >= 8 * p), piece, 0.0))
    matrix = jnp.concatenate(pieces, axis=0)
    lane = iota((ROWS, LANES), 1)
    half = lane < 32
    turned = jnp.concatenate([matrix, jnp.zeros((LANES - ROWS, LANES), jnp.float32)], axis=0).T
    turned = jnp.where(half, turned[0:ROWS], pltpu.roll(turned[ROWS : 2 * ROWS], 32, 1))
    below = (lane < 64) & (((lane & 31) >> 3) < (iota((ROWS, LANES), 0) >> 3))
    matrix = jnp.where(below, turned, matrix)
    row_lane = iota((1, LANES), 1)
    order = basis_rows()
    for start in range(0, len(order), SOLVE_BLOCK):
        block = order[start : start + SOLVE_BLOCK]
        columns = [jnp.where(half, matrix[:, k : k + 1], matrix[:, 32 + k : 33 + k]) for k in block]
        for j, k in enumerate(block):
            scaled = columns[j] / jnp.broadcast_to(columns[j][k : k + 1, :], (ROWS, LANES))
            for i in range(j + 1, len(block)):
                columns[i] = columns[i] - scaled * columns[i][k : k + 1, :]
            matrix = jnp.where((lane & 31) == k, scaled, matrix - scaled * matrix[k : k + 1, :])
    answer = matrix[SCIENCE_ROW : SCIENCE_ROW + 1, :]
    valid = row_lane < 0
    for k in basis_rows():
        valid = valid | ((row_lane & 31) == k)
    answer = jnp.where(valid & (row_lane < 64), answer, 0.0)
    for n in range(out.shape[0]):
        out[n] = answer


def model_kernel(details, answers, images, model, wide, sums):
    turned = jnp.concatenate([answers[...], jnp.zeros((LANES - 8, LANES), jnp.float32)], axis=0).T
    for v in range(VIS_DEV):
        piece = turned[(v % 2) * ROWS : (v % 2) * ROWS + ROWS, v // 2 : v // 2 + 1]
        wide[v] = jnp.broadcast_to(piece, (ROWS, LANES))
    block = 16

    def step(g, carry):
        near = images.at[pl.ds(pl.multiple_of(g * block * ROWS, block * ROWS), block * ROWS), :]
        for t in range(block):
            v = details[t % 2, 0, g * (block // 2) + t // 2]
            scale = [wide[v, 8 * m : 8 * m + 8] for m in range(4)]
            first = t * ROWS
            for i in range(2):
                lanes = slice(i * LANES, (i + 1) * LANES)
                acc = scale[0] * near[first : first + 8, lanes]
                for m in range(1, 4):
                    acc = acc + scale[m] * near[first + 8 * m : first + 8 * m + 8, lanes]
                sums[(2 * t + i) * 8 : (2 * t + i) * 8 + 8, :] = acc
        out = sums[pl.ds(0, 2 * block, stride=8), :]
        for n in range(1, 8):
            out = out + sums[pl.ds(n, 2 * block, stride=8), :]
        model[pl.ds(pl.multiple_of(g * 2 * block, 2 * block), 2 * block), :] = out.astype(jnp.bfloat16)
        return carry

    lax.fori_loop(0, 2 * LANES // block, step, 0)


def order_kernel(answers, out):
    row, place = iota((LANES, NB), 0), iota((LANES, NB), 1)
    for h in range(2):
        chosen = row < 0
        for k, at in enumerate(basis_rows()):
            chosen = chosen | ((place == k) & (row == 32 * h + at))
        out[pl.ds(h, 8, stride=2), :] = jnp.dot(
            answers[...], jnp.where(chosen, 1.0, 0.0), precision=lax.Precision.HIGHEST,
            preferred_element_type=jnp.float32)


def final_kernel(slots, science, returned, out):
    column = jnp.broadcast_to(slots[0:1, :], (LANES, LANES)).T
    column = jnp.concatenate([column] * 4, axis=1)
    for i in range(2):
        chosen = iota((LANES, 4 * LANES), 1) == column * 2 + i
        chosen = jnp.where(chosen, 1.0, 0.0).astype(jnp.bfloat16)
        model = jnp.dot(chosen, returned[...], preferred_element_type=jnp.float32)
        out[pl.ds(i, LANES, stride=2), :] = science[pl.ds(i, LANES, stride=2), :] - model


def vmem(count):
    return [pl.BlockSpec(memory_space=pltpu.VMEM)] * count


def shape(dims, dtype=jnp.float32):
    return jax.ShapeDtypeStruct(dims, dtype)


def params(mebibytes):
    return pltpu.CompilerParams(vmem_limit_bytes=mebibytes << 20)


def pack(science, sigma, dest, visit, offsets):
    return pl.pallas_call(
        pack_kernel,
        out_shape=(shape((LANES * SLOT_ROWS, LANES), jnp.bfloat16), shape((8, LANES), jnp.int32)),
        in_specs=vmem(5), out_specs=tuple(vmem(2)),
        scratch_shapes=[pltpu.VMEM((5 * LANES, LANES), jnp.bfloat16)],
        compiler_params=params(60), name="pack",
    )(science, sigma, dest, visit, offsets)


def keep(place, parts, tables):
    return pl.pallas_call(
        keep_kernel,
        out_shape=(shape((256, 1024), jnp.bfloat16),) + tuple(shape(t.shape, t.dtype) for t in tables),
        in_specs=[pl.BlockSpec(memory_space=pltpu.SMEM)] + vmem(7), out_specs=tuple(vmem(4)),
        compiler_params=params(8), name="keep",
    )(place, *parts, *tables)


def fit(arrived, template, band, wide_p, wide_q):
    return pl.pallas_call(
        fit_kernel,
        out_shape=(shape((2 * LANES * ROWS, 2 * LANES)), shape((VIS_DEV * 5, LANES)),
                   shape((2, 8, LANES), jnp.int32)),
        in_specs=vmem(5), out_specs=tuple(vmem(3)),
        scratch_shapes=[
            pltpu.VMEM((236 * 9 * 2, 16, LANES), jnp.bfloat16),
            pltpu.VMEM((LANES * SLOT_ROWS, LANES), jnp.float32),
            pltpu.VMEM((2, GROUP * 16, 256), jnp.bfloat16), pltpu.VMEM((2, GROUP * 16, 256), jnp.bfloat16),
            pltpu.VMEM((2, GROUP * 16, len(COLS_P) * LANES), jnp.float32),
            pltpu.VMEM((2, GROUP * 16, len(COLS_Q) * LANES), jnp.float32),
            pltpu.VMEM((2, GROUP * ROWS, 256), jnp.bfloat16),
            pltpu.VMEM((VIS_DEV, ROWS, LANES), jnp.float32),
            pltpu.SMEM((2, 8, LANES), jnp.int32), pltpu.SemaphoreType.DMA,
        ],
        compiler_params=params(40), name="fit",
    )(arrived, template, band, wide_p, wide_q)


def middle(parts):
    return pl.pallas_call(middle_kernel, out_shape=shape((2 * parts.shape[0], LANES)),
                          in_specs=vmem(1), out_specs=vmem(1)[0], compiler_params=params(4), name="middle")(parts)


def solve(parts):
    return pl.pallas_call(solve_kernel, out_shape=shape((8, 1, LANES)),
                          in_specs=vmem(1), out_specs=vmem(1)[0], compiler_params=params(4), name="solve")(parts)


def model_of(details, answers, images):
    return pl.pallas_call(
        model_kernel,
        out_shape=shape((4 * LANES, LANES), jnp.bfloat16),
        in_specs=[pl.BlockSpec(memory_space=pltpu.SMEM)] + vmem(2),
        out_specs=vmem(1)[0],
        scratch_shapes=[pltpu.VMEM((VIS_DEV, ROWS, LANES), jnp.float32),
                        pltpu.VMEM((16 * 16, LANES), jnp.float32)],
        compiler_params=params(14), name="model",
    )(details, answers, images)


def order(answers):
    return pl.pallas_call(order_kernel, out_shape=shape((VIS_DEV, NB)), in_specs=vmem(1),
                          out_specs=vmem(1)[0], compiler_params=params(4), name="order")(answers)


def final(slots, science, returned):
    return pl.pallas_call(final_kernel, out_shape=shape((2 * LANES, LANES)),
                          in_specs=vmem(3), out_specs=vmem(1)[0], compiler_params=params(4), name="final")(slots, science, returned)


def exchange(values, groups=None):
    return lax.all_to_all(values, "patch", split_axis=0, concat_axis=0, tiled=True,
                          axis_index_groups=groups)


def per_device(science, inverse_sigma, template, destination, offsets, visit_local):
    patches = lax.axis_size("patch")
    planes = [[z * 8 + i for i in range(8)] for z in range(patches // 8)]
    lines = [[z * 8 + i for z in range(patches // 8)] for i in range(8)]
    own = template[0].astype(jnp.bfloat16)
    parts = [own] + [lax.ppermute(own, "visit", [(x, x ^ m) for x in range(4)]) for m in (1, 2, 3)]
    place = lax.axis_index("visit").astype(jnp.int32).reshape(1)
    science_rows = science.reshape(2 * LANES, LANES)
    packed, slots = pack(science_rows, inverse_sigma.reshape(2 * LANES, LANES),
                         destination.reshape(1, LANES), visit_local.reshape(1, LANES), offsets.T)
    kept = keep(place, parts, constants())
    arrived = exchange(packed.reshape(patches, 5, 2, LANES)).reshape(LANES * SLOT_ROWS, LANES)
    images, gram, details = fit(arrived, *kept)
    parts = exchange(gram.reshape(8, 5, 2, LANES), planes).reshape(gram.shape)
    parts = exchange(middle(parts).reshape(16, 5, 2, LANES), lines).reshape(160, LANES)
    answers = exchange(solve(parts), planes).reshape(8, LANES)
    model = model_of(details, answers, images)
    returned = exchange(model.reshape(patches, 2, 2, LANES)).reshape(4 * LANES, LANES)
    difference = final(slots, science_rows, returned)
    coefficients = order(answers)
    return difference.reshape(science.shape), coefficients


def solution(mesh):
    return jax.shard_map(
        per_device,
        mesh=mesh,
        in_specs=(
            P(("patch", "visit"), None, None),
            P(("patch", "visit"), None, None),
            P("patch", "visit", None),
            P(("patch", "visit")),
            P(("patch", "visit"), None),
            P(("patch", "visit")),
        ),
        out_specs=(P(("patch", "visit"), None, None), P("visit", None)),
        check_vma=False,
    )
```

```python
import functools

import jax
import jax.numpy as jnp
import numpy as np
from jax import lax
from jax.experimental import pallas as pl
from jax.experimental.pallas import tpu as pltpu
from jax.sharding import PartitionSpec as P

KR = 10
TAPS = 2 * KR + 1
NB = 28
VIS_DEV = 16
ROWS = 32
LANES = 128
GROUP = 16
DEPTH = 160
SOLVE_BLOCK = 7
FILTER_ROWS = 80
FILTER_BAND = 656
FILTER_DEPTH = 112
SLOT_ROWS = 10

gauss_widths = (1.0, 2.0, 4.0)
poly_degrees = (4, 2, 2)

SET_P = (0, 1, 2, 3, 4, 5, 6, 7)
SET_Q = (8, 9, 10, 0, 1, 0, 8, 9)
COLS_P = (0, 1, 2, 5, 6, 7)
COLS_Q = (8, 3, 4, 9, 10)

ROW_PAIRS = (
    [(0, b) for b in range(5)] + [(5, 5), (5, 6), (5, 7)]
    + [(1, b) for b in range(4)] + [None, (6, 5), (6, 6), None]
    + [(2, 0), (2, 1), (2, 2), None, None, (7, 5), (10, 8), None]
    + [(8, 8), (8, 9), (8, 10), (3, 0), (3, 1), (4, 0), (9, 8), (9, 9)]
)
WEIGHT_ROW = 12
SCIENCE_ROW = 15


def filter_table(radius):
    tap_points = np.arange(-radius, radius + 1) * 1.0
    raw_columns = []
    for width_value, degree in zip(gauss_widths, poly_degrees):
        bell_curve = np.exp(-tap_points * tap_points / (2.0 * width_value * width_value))
        for power_index in range(degree + 1):
            raw_columns.append(bell_curve * (tap_points / radius) ** power_index)
    orthonormal = []
    for column in raw_columns:
        vector = column.copy()
        for repeat_index in range(2):
            for earlier in orthonormal:
                vector = vector - np.dot(earlier, vector) * earlier
        orthonormal.append(vector / np.sqrt(np.dot(vector, vector)))
    return np.stack(orthonormal, axis=1).astype(np.float32)


def basis_rows():
    rows = []
    offset = 0
    for degree in poly_degrees:
        for first in range(degree + 1):
            for second in range(degree + 1 - first):
                rows.append(ROW_PAIRS.index((offset + first, offset + second)))
        offset += degree + 1
    return rows + [WEIGHT_ROW]


def constants():
    values = filter_table(KR)
    band = np.zeros((2 * FILTER_BAND, FILTER_DEPTH), np.float32)
    for which, held in enumerate((SET_P, SET_Q)):
        for y in range(FILTER_ROWS + 1):
            for row, b in enumerate(held):
                band[which * FILTER_BAND + y * 8 + row, y : y + TAPS] = values[:, b]
    columns = []
    for held in (COLS_P, COLS_Q):
        wide = np.zeros((DEPTH, len(held) * LANES), np.float32)
        for place, a in enumerate(held):
            for j in range(LANES):
                wide[j : j + TAPS, place * LANES + j] = values[:, a]
        columns.append(wide)
    return [jnp.asarray(c).astype(jnp.bfloat16) for c in (band, *columns)]


def iota(shape, axis):
    return lax.broadcasted_iota(jnp.int32, shape, axis)


def pack_kernel(science, sigma, dest, visit, offsets, packed, slots, stack):
    d = jnp.broadcast_to(dest[...], (LANES, LANES))
    earlier = (d.T == d) & (iota(d.shape, 0) < iota(d.shape, 1))
    rank = jnp.sum(jnp.where(earlier, 1, 0), axis=0, keepdims=True)
    slots[...] = jnp.broadcast_to(dest[...] * 2 + rank, slots.shape)
    for i in range(2):
        weight = sigma[pl.ds(i, LANES, stride=2), :]
        scaled = science[pl.ds(i, LANES, stride=2), :] * weight
        stack[i * LANES : (i + 1) * LANES, :] = scaled.astype(jnp.bfloat16)
        stack[(2 + i) * LANES : (3 + i) * LANES, :] = weight.astype(jnp.bfloat16)
    column = offsets[1:2, :]
    fields = (visit[...], offsets[0:1, :], column >> 7, column & 127)
    row = iota((LANES, LANES), 0)
    details = jnp.zeros((LANES, LANES), jnp.float32)
    for place, field in enumerate(fields):
        details = jnp.where(row == place, field.astype(jnp.float32), details)
    stack[4 * LANES :, :] = details.T.astype(jnp.bfloat16)
    first = dest[...] * SLOT_ROWS
    targets = (first + 2 * rank, first + 2 * rank + 1, first + 4 + 2 * rank,
               first + 5 + 2 * rank, first + 8 + rank)
    target = jnp.concatenate(targets, axis=1)
    block = 256
    for start in range(0, packed.shape[0], block):
        chosen = iota((block, 5 * LANES), 0) + start == target
        chosen = jnp.where(chosen, 1.0, 0.0).astype(jnp.bfloat16)
        packed[start : start + block, :] = jnp.dot(
            chosen, stack[...], preferred_element_type=jnp.float32
        ).astype(jnp.bfloat16)


def keep_kernel(place, own, next_1, next_2, next_3, band, wide_p, wide_q,
                template, kept_band, kept_p, kept_q):
    for m, part in enumerate((own, next_1, next_2, next_3)):
        at = pl.multiple_of((place[0] ^ m) * 64, 64)
        template[pl.ds(at, 64), :] = part[...]
    kept_band[...] = band[...]
    kept_p[...] = wide_p[...]
    kept_q[...] = wide_q[...]


def fit_kernel(arrived, template, band, wide_p, wide_q, images, gram, details_out,
               rows, data, left_p, left_q, right_p, right_q, design,
               total, details, sem):
    data[...] = arrived[...].astype(jnp.float32)
    for c in range(2):
        fields = data[pl.ds(8 + c, LANES, stride=SLOT_ROWS), :].T[0:8, :].astype(jnp.int32)
        line = iota((8, LANES), 0)
        at = (fields[1:2, :] * 9 + fields[2:3, :]) * 2
        turn = (LANES - fields[3:4, :]) & 127
        fields = jnp.where(line == 1, at, jnp.where(line == 2, turn, fields))
        details_out[c] = fields
    copy = pltpu.make_async_copy(details_out, details, sem)
    copy.start()
    for y0 in range(0, 240, FILTER_ROWS):
        depth = min(FILTER_DEPTH, 256 - y0)
        made = jnp.dot(band[:, 0:depth], template[y0 : y0 + depth, :],
                       preferred_element_type=jnp.float32)
        for which in range(2):
            for y in range(FILTER_ROWS):
                if y0 + y < 236:
                    first = which * FILTER_BAND + y * 8
                    pair = made[first : first + 16, :].astype(jnp.bfloat16)
                    for tile in range(8):
                        rows[((y0 + y) * 9 + tile) * 2 + which] = pair[:, tile * LANES : (tile + 1) * LANES]
    empty = jnp.zeros((16, LANES), jnp.bfloat16)
    for y in range(236):
        for which in range(2):
            rows[(y * 9 + 8) * 2 + which] = empty
    total[...] = jnp.zeros_like(total)
    copy.wait()
    lane = iota((16, LANES), 1)
    sub = iota((8, LANES), 0)
    quarter = iota((ROWS, LANES), 1) >> 5
    groups = 2 * LANES // GROUP

    def gather(g, side):
        for t in range(GROUP):
            c = t % 2
            src = g * (GROUP // 2) + t // 2
            at = details[c, 1, src]
            back = details[c, 2, src]
            keep = lane < LANES - details[c, 3, src]
            for which, left in enumerate((left_p, left_q)):
                turned = [pltpu.roll(rows[at + 2 * m + which], back, 1) for m in range(3)]
                for m in range(2):
                    left[side, t * 16 : t * 16 + 16, m * LANES : (m + 1) * LANES] = jnp.where(
                        keep, turned[m], turned[m + 1]
                    )

    def filter_columns(side):
        right_p[side] = jnp.dot(left_p[side, :, 0:DEPTH], wide_p[...], preferred_element_type=jnp.float32)
        right_q[side] = jnp.dot(left_q[side, :, 0:DEPTH], wide_q[...], preferred_element_type=jnp.float32)

    def combine(g, side):
        for t in range(GROUP):
            c = t % 2
            src = g * (GROUP // 2) + t // 2
            for i in range(2):
                at = t * 16 + i * 8

                def p(a):
                    k = COLS_P.index(a)
                    return right_p[side, at : at + 8, k * LANES : (k + 1) * LANES]

                def q(a):
                    k = COLS_Q.index(a)
                    return right_q[side, at : at + 8, k * LANES : (k + 1) * LANES]

                v0 = jnp.where(sub < 5, p(0), p(5))
                v1 = jnp.where(sub < 4, p(1), jnp.where(sub == 7, 0.0, p(6)))
                v1 = jnp.where(sub == 4, 1.0, v1)
                v2 = jnp.where(sub < 3, p(2), jnp.where(sub == 5, p(7), jnp.where(sub == 6, q(10), 0.0)))
                v3 = jnp.where(sub < 3, q(8), jnp.where(sub < 5, q(3), jnp.where(sub < 6, q(4), q(9))))
                lanes = slice(i * LANES, (i + 1) * LANES)
                first = pl.multiple_of((g * GROUP + t) * ROWS, ROWS)
                for m, v in enumerate((v0, v1, v2, v3)):
                    images[pl.ds(first + 8 * m, 8), lanes] = v
                weight = data[pl.ds(src * SLOT_ROWS + 4 + 2 * c + i, 1), :]
                science = data[pl.ds(src * SLOT_ROWS + 2 * c + i, 1), :]
                d1 = jnp.where(sub == 7, science, v1 * weight)
                whole = jnp.concatenate([v0 * weight, d1, v2 * weight, v3 * weight], axis=0)
                design[side, t * ROWS : (t + 1) * ROWS, lanes] = whole.astype(jnp.bfloat16)

    def accumulate(g, side):
        for h in range(GROUP // 4):
            part = design[side, h * 128 : (h + 1) * 128, :]
            product = lax.dot_general(part, part, (((1,), (1,)), ((), ())),
                                      preferred_element_type=jnp.float32)
            for n in range(4):
                t = h * 4 + n
                v = details[t % 2, 0, g * (GROUP // 2) + t // 2]
                total[v] += jnp.where(quarter == n, product[n * ROWS : (n + 1) * ROWS, :], 0.0)

    def step(j, carry):
        for side in range(2):
            g = 2 * j + side
            accumulate(g - 2, side)
            combine(g - 1, 1 - side)
            filter_columns(side)
            gather(jnp.minimum(g + 1, groups - 1), 1 - side)
        return carry

    gather(0, 0)
    filter_columns(0)
    gather(1, 1)
    combine(0, 0)
    filter_columns(1)
    gather(2, 0)
    lax.fori_loop(1, groups // 2, step, 0)
    accumulate(groups - 2, 0)
    combine(groups - 1, 1)
    accumulate(groups - 1, 1)
    lane8 = iota((8, LANES), 1)
    line = lane8[0:2] >> 5
    for c in range(VIS_DEV // 2):
        sums = []
        for v in (2 * c, 2 * c + 1):
            whole = total[v]
            whole = whole + pltpu.roll(whole, 64, 1)
            sums.append(whole + pltpu.roll(whole, 32, 1))
        first, second = ([w[8 * p : 8 * p + 8] for p in range(4)] for w in sums)
        upper = [jnp.where(lane8 < 64, x, y) for x, y in zip(first, second)]
        place = lane8 & 63
        main = jnp.where(place < 32, upper[0], upper[1])
        gram[10 * c : 10 * c + 8, :] = jnp.where(
            (place >= 32) & (place < 40),
            jnp.where(lane8 < 64, pltpu.roll(first[3], 8, 1), pltpu.roll(second[3], 8, 1)), main)
        extra = jnp.where((lane8 & 31) < 16, pltpu.roll(first[2], 16, 1), second[2])
        low = jnp.where(line == 0, extra[0:2], extra[2:4])
        high = jnp.where(line == 2, extra[4:6], extra[6:8])
        gram[10 * c + 8 : 10 * c + 10, :] = jnp.where(line < 2, low, high)


def total_of(parts):
    main, extra = parts[0:8, :], parts[8:10, :]
    for n in range(10, parts.shape[0], 10):
        main = main + parts[n : n + 8, :]
        extra = extra + parts[n + 8 : n + 10, :]
    return main, extra


def middle_kernel(parts, out):
    main, extra = total_of(parts)
    for n in range(4):
        out[n] = main[2 * n : 2 * n + 2]
    out[4] = extra


def solve_kernel(parts, out):
    main, extra = total_of(parts)
    rest = jnp.concatenate([extra if m == 0 else pltpu.roll(extra, 128 - 32 * m, 1) for m in range(4)], axis=0)
    lane8 = iota((8, LANES), 1)
    turns = ((main, 0, 96), (main, 96, 64), (rest, 16, 32), (main, 120, 88))
    pieces = []
    for p, (source, near, far) in enumerate(turns):
        near = pltpu.roll(source, near, 1) if near else source
        piece = jnp.where(lane8 < 32, near, pltpu.roll(source, far, 1))
        pieces.append(jnp.where((lane8 < 64) & ((lane8 & 31) >= 8 * p), piece, 0.0))
    matrix = jnp.concatenate(pieces, axis=0)
    lane = iota((ROWS, LANES), 1)
    half = lane < 32
    turned = jnp.concatenate([matrix, jnp.zeros((LANES - ROWS, LANES), jnp.float32)], axis=0).T
    turned = jnp.where(half, turned[0:ROWS], pltpu.roll(turned[ROWS : 2 * ROWS], 32, 1))
    below = (lane < 64) & (((lane & 31) >> 3) < (iota((ROWS, LANES), 0) >> 3))
    matrix = jnp.where(below, turned, matrix)
    row_lane = iota((1, LANES), 1)
    order = basis_rows()
    for start in range(0, len(order), SOLVE_BLOCK):
        block = order[start : start + SOLVE_BLOCK]
        columns = [jnp.where(half, matrix[:, k : k + 1], matrix[:, 32 + k : 33 + k]) for k in block]
        for j, k in enumerate(block):
            scaled = columns[j] / jnp.broadcast_to(columns[j][k : k + 1, :], (ROWS, LANES))
            for i in range(j + 1, len(block)):
                columns[i] = columns[i] - scaled * columns[i][k : k + 1, :]
            matrix = jnp.where((lane & 31) == k, scaled, matrix - scaled * matrix[k : k + 1, :])
    answer = matrix[SCIENCE_ROW : SCIENCE_ROW + 1, :]
    valid = row_lane < 0
    for k in basis_rows():
        valid = valid | ((row_lane & 31) == k)
    answer = jnp.where(valid & (row_lane < 64), answer, 0.0)
    for n in range(out.shape[0]):
        out[n] = answer


def model_kernel(details, answers, images, model, wide, sums):
    turned = jnp.concatenate([answers[...], jnp.zeros((LANES - 8, LANES), jnp.float32)], axis=0).T
    for v in range(VIS_DEV):
        piece = turned[(v % 2) * ROWS : (v % 2) * ROWS + ROWS, v // 2 : v // 2 + 1]
        wide[v] = jnp.broadcast_to(piece, (ROWS, LANES))
    block = 16

    def step(g, carry):
        near = images.at[pl.ds(pl.multiple_of(g * block * ROWS, block * ROWS), block * ROWS), :]
        for t in range(block):
            v = details[t % 2, 0, g * (block // 2) + t // 2]
            scale = [wide[v, 8 * m : 8 * m + 8] for m in range(4)]
            first = t * ROWS
            for i in range(2):
                lanes = slice(i * LANES, (i + 1) * LANES)
                acc = scale[0] * near[first : first + 8, lanes]
                for m in range(1, 4):
                    acc = acc + scale[m] * near[first + 8 * m : first + 8 * m + 8, lanes]
                sums[(2 * t + i) * 8 : (2 * t + i) * 8 + 8, :] = acc
        out = sums[pl.ds(0, 2 * block, stride=8), :]
        for n in range(1, 8):
            out = out + sums[pl.ds(n, 2 * block, stride=8), :]
        model[pl.ds(pl.multiple_of(g * 2 * block, 2 * block), 2 * block), :] = out.astype(jnp.bfloat16)
        return carry

    lax.fori_loop(0, 2 * LANES // block, step, 0)


def order_kernel(answers, out):
    row, place = iota((LANES, NB), 0), iota((LANES, NB), 1)
    for h in range(2):
        chosen = row < 0
        for k, at in enumerate(basis_rows()):
            chosen = chosen | ((place == k) & (row == 32 * h + at))
        out[pl.ds(h, 8, stride=2), :] = jnp.dot(
            answers[...], jnp.where(chosen, 1.0, 0.0), precision=lax.Precision.HIGHEST,
            preferred_element_type=jnp.float32)


def final_kernel(slots, science, returned, out):
    column = jnp.broadcast_to(slots[0:1, :], (LANES, LANES)).T
    column = jnp.concatenate([column] * 4, axis=1)
    for i in range(2):
        chosen = iota((LANES, 4 * LANES), 1) == column * 2 + i
        chosen = jnp.where(chosen, 1.0, 0.0).astype(jnp.bfloat16)
        model = jnp.dot(chosen, returned[...], preferred_element_type=jnp.float32)
        out[pl.ds(i, LANES, stride=2), :] = science[pl.ds(i, LANES, stride=2), :] - model


def vmem(count):
    return [pl.BlockSpec(memory_space=pltpu.VMEM)] * count


def shape(dims, dtype=jnp.float32):
    return jax.ShapeDtypeStruct(dims, dtype)


def params(mebibytes):
    return pltpu.CompilerParams(vmem_limit_bytes=mebibytes << 20)


def pack(science, sigma, dest, visit, offsets):
    return pl.pallas_call(
        pack_kernel,
        out_shape=(shape((LANES * SLOT_ROWS, LANES), jnp.bfloat16), shape((8, LANES), jnp.int32)),
        in_specs=vmem(5), out_specs=tuple(vmem(2)),
        scratch_shapes=[pltpu.VMEM((5 * LANES, LANES), jnp.bfloat16)],
        compiler_params=params(60), name="pack",
    )(science, sigma, dest, visit, offsets)


def keep(place, parts, tables):
    return pl.pallas_call(
        keep_kernel,
        out_shape=(shape((256, 1024), jnp.bfloat16),) + tuple(shape(t.shape, t.dtype) for t in tables),
        in_specs=[pl.BlockSpec(memory_space=pltpu.SMEM)] + vmem(7), out_specs=tuple(vmem(4)),
        compiler_params=params(8), name="keep",
    )(place, *parts, *tables)


def fit(arrived, template, band, wide_p, wide_q):
    return pl.pallas_call(
        fit_kernel,
        out_shape=(shape((2 * LANES * ROWS, 2 * LANES)), shape((VIS_DEV * 5, LANES)),
                   shape((2, 8, LANES), jnp.int32)),
        in_specs=vmem(5), out_specs=tuple(vmem(3)),
        scratch_shapes=[
            pltpu.VMEM((236 * 9 * 2, 16, LANES), jnp.bfloat16),
            pltpu.VMEM((LANES * SLOT_ROWS, LANES), jnp.float32),
            pltpu.VMEM((2, GROUP * 16, 256), jnp.bfloat16), pltpu.VMEM((2, GROUP * 16, 256), jnp.bfloat16),
            pltpu.VMEM((2, GROUP * 16, len(COLS_P) * LANES), jnp.float32),
            pltpu.VMEM((2, GROUP * 16, len(COLS_Q) * LANES), jnp.float32),
            pltpu.VMEM((2, GROUP * ROWS, 256), jnp.bfloat16),
            pltpu.VMEM((VIS_DEV, ROWS, LANES), jnp.float32),
            pltpu.SMEM((2, 8, LANES), jnp.int32), pltpu.SemaphoreType.DMA,
        ],
        compiler_params=params(40), name="fit",
    )(arrived, template, band, wide_p, wide_q)


def middle(parts):
    return pl.pallas_call(middle_kernel, out_shape=shape((5, 2, LANES)),
                          in_specs=vmem(1), out_specs=vmem(1)[0], compiler_params=params(4), name="middle")(parts)


def solve(parts):
    return pl.pallas_call(solve_kernel, out_shape=shape((8, 1, LANES)),
                          in_specs=vmem(1), out_specs=vmem(1)[0], compiler_params=params(4), name="solve")(parts)


def model_of(details, answers, images):
    return pl.pallas_call(
        model_kernel,
        out_shape=shape((4 * LANES, LANES), jnp.bfloat16),
        in_specs=[pl.BlockSpec(memory_space=pltpu.SMEM)] + vmem(2),
        out_specs=vmem(1)[0],
        scratch_shapes=[pltpu.VMEM((VIS_DEV, ROWS, LANES), jnp.float32),
                        pltpu.VMEM((16 * 16, LANES), jnp.float32)],
        compiler_params=params(14), name="model",
    )(details, answers, images)


def order(answers):
    return pl.pallas_call(order_kernel, out_shape=shape((VIS_DEV, NB)), in_specs=vmem(1),
                          out_specs=vmem(1)[0], compiler_params=params(4), name="order")(answers)


def final(slots, science, returned):
    return pl.pallas_call(final_kernel, out_shape=shape((2 * LANES, LANES)),
                          in_specs=vmem(3), out_specs=vmem(1)[0], compiler_params=params(4), name="final")(slots, science, returned)


def exchange(values, groups=None):
    return lax.all_to_all(values, "patch", split_axis=0, concat_axis=0, tiled=True,
                          axis_index_groups=groups)


def per_device(science, inverse_sigma, template, destination, offsets, visit_local):
    patches = lax.axis_size("patch")
    planes = [[z * 8 + i for i in range(8)] for z in range(patches // 8)]
    lines = [[z * 8 + i for z in range(patches // 8)] for i in range(8)]
    own = template[0].astype(jnp.bfloat16)
    parts = [own] + [lax.ppermute(own, "visit", [(x, x ^ m) for x in range(4)]) for m in (1, 2, 3)]
    place = lax.axis_index("visit").astype(jnp.int32).reshape(1)
    science_rows = science.reshape(2 * LANES, LANES)
    packed, slots = pack(science_rows, inverse_sigma.reshape(2 * LANES, LANES),
                         destination.reshape(1, LANES), visit_local.reshape(1, LANES), offsets.T)
    kept = keep(place, parts, constants())
    arrived = exchange(packed.reshape(patches, 5, 2, LANES)).reshape(LANES * SLOT_ROWS, LANES)
    images, gram, details = fit(arrived, *kept)
    parts = exchange(gram.reshape(8, 5, 2, LANES), planes).reshape(gram.shape)
    parts = lax.all_gather(middle(parts), "patch", axis_index_groups=lines)
    parts = parts.reshape(160, LANES)
    answers = exchange(solve(parts), planes).reshape(8, LANES)
    model = model_of(details, answers, images)
    returned = exchange(model.reshape(patches, 2, 2, LANES)).reshape(4 * LANES, LANES)
    difference = final(slots, science_rows, returned)
    coefficients = order(answers)
    return difference.reshape(science.shape), coefficients


def solution(mesh):
    return jax.shard_map(
        per_device,
        mesh=mesh,
        in_specs=(
            P(("patch", "visit"), None, None),
            P(("patch", "visit"), None, None),
            P("patch", "visit", None),
            P(("patch", "visit")),
            P(("patch", "visit"), None),
            P(("patch", "visit")),
        ),
        out_specs=(P(("patch", "visit"), None, None), P("visit", None)),
        check_vma=False,
    )
```

```python
import functools

import jax
import jax.numpy as jnp
import numpy as np
from jax import lax
from jax.experimental import pallas as pl
from jax.experimental.pallas import tpu as pltpu
from jax.sharding import PartitionSpec as P

KR = 10
TAPS = 2 * KR + 1
NB = 28
VIS_DEV = 16
ROWS = 32
LANES = 128
GROUP = 32
DEPTH = 160
SOLVE_BLOCK = 7
FILTER_ROWS = 80
FILTER_BAND = 656
FILTER_DEPTH = 112
SLOT_ROWS = 10

gauss_widths = (1.0, 2.0, 4.0)
poly_degrees = (4, 2, 2)

SET_P = (0, 1, 2, 3, 4, 5, 6, 7)
SET_Q = (8, 9, 10, 0, 1, 0, 8, 9)
COLS_P = (0, 1, 2, 5, 6, 7)
COLS_Q = (8, 3, 4, 9, 10)

ROW_PAIRS = (
    [(0, b) for b in range(5)] + [(5, 5), (5, 6), (5, 7)]
    + [(1, b) for b in range(4)] + [None, (6, 5), (6, 6), None]
    + [(2, 0), (2, 1), (2, 2), None, None, (7, 5), (10, 8), None]
    + [(8, 8), (8, 9), (8, 10), (3, 0), (3, 1), (4, 0), (9, 8), (9, 9)]
)
WEIGHT_ROW = 12
SCIENCE_ROW = 15


def filter_table(radius):
    tap_points = np.arange(-radius, radius + 1) * 1.0
    raw_columns = []
    for width_value, degree in zip(gauss_widths, poly_degrees):
        bell_curve = np.exp(-tap_points * tap_points / (2.0 * width_value * width_value))
        for power_index in range(degree + 1):
            raw_columns.append(bell_curve * (tap_points / radius) ** power_index)
    orthonormal = []
    for column in raw_columns:
        vector = column.copy()
        for repeat_index in range(2):
            for earlier in orthonormal:
                vector = vector - np.dot(earlier, vector) * earlier
        orthonormal.append(vector / np.sqrt(np.dot(vector, vector)))
    return np.stack(orthonormal, axis=1).astype(np.float32)


def basis_rows():
    rows = []
    offset = 0
    for degree in poly_degrees:
        for first in range(degree + 1):
            for second in range(degree + 1 - first):
                rows.append(ROW_PAIRS.index((offset + first, offset + second)))
        offset += degree + 1
    return rows + [WEIGHT_ROW]


def constants():
    values = filter_table(KR)
    band = np.zeros((2 * FILTER_BAND, FILTER_DEPTH), np.float32)
    for which, held in enumerate((SET_P, SET_Q)):
        for y in range(FILTER_ROWS + 1):
            for row, b in enumerate(held):
                band[which * FILTER_BAND + y * 8 + row, y : y + TAPS] = values[:, b]
    columns = []
    for held in (COLS_P, COLS_Q):
        wide = np.zeros((DEPTH, len(held) * LANES), np.float32)
        for place, a in enumerate(held):
            for j in range(LANES):
                wide[j : j + TAPS, place * LANES + j] = values[:, a]
        columns.append(wide)
    return [jnp.asarray(c).astype(jnp.bfloat16) for c in (band, *columns)]


def iota(shape, axis):
    return lax.broadcasted_iota(jnp.int32, shape, axis)


def pack_kernel(science, sigma, dest, visit, offsets, packed, slots, stack):
    d = jnp.broadcast_to(dest[...], (LANES, LANES))
    earlier = (d.T == d) & (iota(d.shape, 0) < iota(d.shape, 1))
    rank = jnp.sum(jnp.where(earlier, 1, 0), axis=0, keepdims=True)
    slots[...] = jnp.broadcast_to(dest[...] * 2 + rank, slots.shape)
    for i in range(2):
        weight = sigma[pl.ds(i, LANES, stride=2), :]
        scaled = science[pl.ds(i, LANES, stride=2), :] * weight
        stack[i * LANES : (i + 1) * LANES, :] = scaled.astype(jnp.bfloat16)
        stack[(2 + i) * LANES : (3 + i) * LANES, :] = weight.astype(jnp.bfloat16)
    column = offsets[1:2, :]
    fields = (visit[...], offsets[0:1, :], column >> 7, column & 127)
    row = iota((LANES, LANES), 0)
    details = jnp.zeros((LANES, LANES), jnp.float32)
    for place, field in enumerate(fields):
        details = jnp.where(row == place, field.astype(jnp.float32), details)
    stack[4 * LANES :, :] = details.T.astype(jnp.bfloat16)
    first = dest[...] * SLOT_ROWS
    targets = (first + 2 * rank, first + 2 * rank + 1, first + 4 + 2 * rank,
               first + 5 + 2 * rank, first + 8 + rank)
    target = jnp.concatenate(targets, axis=1)
    block = 256
    for start in range(0, packed.shape[0], block):
        chosen = iota((block, 5 * LANES), 0) + start == target
        chosen = jnp.where(chosen, 1.0, 0.0).astype(jnp.bfloat16)
        packed[start : start + block, :] = jnp.dot(
            chosen, stack[...], preferred_element_type=jnp.float32
        ).astype(jnp.bfloat16)


def keep_kernel(place, own, next_1, next_2, next_3, band, wide_p, wide_q,
                template, kept_band, kept_p, kept_q):
    for m, part in enumerate((own, next_1, next_2, next_3)):
        at = pl.multiple_of((place[0] ^ m) * 64, 64)
        template[pl.ds(at, 64), :] = part[...]
    kept_band[...] = band[...]
    kept_p[...] = wide_p[...]
    kept_q[...] = wide_q[...]


def fit_kernel(arrived, template, band, wide_p, wide_q, images, gram, details_out,
               rows, data, left_p, left_q, right_p, right_q, design,
               total, details, sem):
    data[...] = arrived[...].astype(jnp.float32)
    for c in range(2):
        fields = data[pl.ds(8 + c, LANES, stride=SLOT_ROWS), :].T[0:8, :].astype(jnp.int32)
        line = iota((8, LANES), 0)
        at = (fields[1:2, :] * 9 + fields[2:3, :]) * 2
        turn = (LANES - fields[3:4, :]) & 127
        fields = jnp.where(line == 1, at, jnp.where(line == 2, turn, fields))
        details_out[c] = fields
    copy = pltpu.make_async_copy(details_out, details, sem)
    copy.start()
    for y0 in range(0, 240, FILTER_ROWS):
        depth = min(FILTER_DEPTH, 256 - y0)
        made = jnp.dot(band[:, 0:depth], template[y0 : y0 + depth, :],
                       preferred_element_type=jnp.float32)
        for which in range(2):
            for y in range(FILTER_ROWS):
                if y0 + y < 236:
                    first = which * FILTER_BAND + y * 8
                    pair = made[first : first + 16, :].astype(jnp.bfloat16)
                    for tile in range(8):
                        rows[((y0 + y) * 9 + tile) * 2 + which] = pair[:, tile * LANES : (tile + 1) * LANES]
    empty = jnp.zeros((16, LANES), jnp.bfloat16)
    for y in range(236):
        for which in range(2):
            rows[(y * 9 + 8) * 2 + which] = empty
    total[...] = jnp.zeros_like(total)
    copy.wait()
    lane = iota((16, LANES), 1)
    sub = iota((8, LANES), 0)
    quarter = iota((ROWS, LANES), 1) >> 5
    groups = 2 * LANES // GROUP

    def gather(g, side):
        for t in range(GROUP):
            c = t % 2
            src = g * (GROUP // 2) + t // 2
            at = details[c, 1, src]
            back = details[c, 2, src]
            keep = lane < LANES - details[c, 3, src]
            for which, left in enumerate((left_p, left_q)):
                turned = [pltpu.roll(rows[at + 2 * m + which], back, 1) for m in range(3)]
                for m in range(2):
                    left[side, t * 16 : t * 16 + 16, m * LANES : (m + 1) * LANES] = jnp.where(
                        keep, turned[m], turned[m + 1]
                    )

    def filter_columns(side):
        right_p[side] = jnp.dot(left_p[side, :, 0:DEPTH], wide_p[...], preferred_element_type=jnp.float32)
        right_q[side] = jnp.dot(left_q[side, :, 0:DEPTH], wide_q[...], preferred_element_type=jnp.float32)

    def combine(g, side):
        for t in range(GROUP):
            c = t % 2
            src = g * (GROUP // 2) + t // 2
            for i in range(2):
                at = t * 16 + i * 8

                def p(a):
                    k = COLS_P.index(a)
                    return right_p[side, at : at + 8, k * LANES : (k + 1) * LANES]

                def q(a):
                    k = COLS_Q.index(a)
                    return right_q[side, at : at + 8, k * LANES : (k + 1) * LANES]

                v0 = jnp.where(sub < 5, p(0), p(5))
                v1 = jnp.where(sub < 4, p(1), jnp.where(sub == 7, 0.0, p(6)))
                v1 = jnp.where(sub == 4, 1.0, v1)
                v2 = jnp.where(sub < 3, p(2), jnp.where(sub == 5, p(7), jnp.where(sub == 6, q(10), 0.0)))
                v3 = jnp.where(sub < 3, q(8), jnp.where(sub < 5, q(3), jnp.where(sub < 6, q(4), q(9))))
                lanes = slice(i * LANES, (i + 1) * LANES)
                first = pl.multiple_of((g * GROUP + t) * ROWS, ROWS)
                for m, v in enumerate((v0, v1, v2, v3)):
                    images[pl.ds(first + 8 * m, 8), lanes] = v
                weight = data[pl.ds(src * SLOT_ROWS + 4 + 2 * c + i, 1), :]
                science = data[pl.ds(src * SLOT_ROWS + 2 * c + i, 1), :]
                d1 = jnp.where(sub == 7, science, v1 * weight)
                whole = jnp.concatenate([v0 * weight, d1, v2 * weight, v3 * weight], axis=0)
                design[side, t * ROWS : (t + 1) * ROWS, lanes] = whole.astype(jnp.bfloat16)

    def accumulate(g, side):
        for h in range(GROUP // 4):
            part = design[side, h * 128 : (h + 1) * 128, :]
            product = lax.dot_general(part, part, (((1,), (1,)), ((), ())),
                                      preferred_element_type=jnp.float32)
            for n in range(4):
                t = h * 4 + n
                v = details[t % 2, 0, g * (GROUP // 2) + t // 2]
                total[v] += jnp.where(quarter == n, product[n * ROWS : (n + 1) * ROWS, :], 0.0)

    def step(j, carry):
        for side in range(2):
            g = 2 * j + side
            accumulate(g - 2, side)
            combine(g - 1, 1 - side)
            filter_columns(side)
            gather(jnp.minimum(g + 1, groups - 1), 1 - side)
        return carry

    gather(0, 0)
    filter_columns(0)
    gather(1, 1)
    combine(0, 0)
    filter_columns(1)
    gather(2, 0)
    lax.fori_loop(1, groups // 2, step, 0)
    accumulate(groups - 2, 0)
    combine(groups - 1, 1)
    accumulate(groups - 1, 1)
    lane8 = iota((8, LANES), 1)
    line = lane8[0:2] >> 5
    for c in range(VIS_DEV // 2):
        sums = []
        for v in (2 * c, 2 * c + 1):
            whole = total[v]
            whole = whole + pltpu.roll(whole, 64, 1)
            sums.append(whole + pltpu.roll(whole, 32, 1))
        first, second = ([w[8 * p : 8 * p + 8] for p in range(4)] for w in sums)
        upper = [jnp.where(lane8 < 64, x, y) for x, y in zip(first, second)]
        place = lane8 & 63
        main = jnp.where(place < 32, upper[0], upper[1])
        gram[10 * c : 10 * c + 8, :] = jnp.where(
            (place >= 32) & (place < 40),
            jnp.where(lane8 < 64, pltpu.roll(first[3], 8, 1), pltpu.roll(second[3], 8, 1)), main)
        extra = jnp.where((lane8 & 31) < 16, pltpu.roll(first[2], 16, 1), second[2])
        low = jnp.where(line == 0, extra[0:2], extra[2:4])
        high = jnp.where(line == 2, extra[4:6], extra[6:8])
        gram[10 * c + 8 : 10 * c + 10, :] = jnp.where(line < 2, low, high)


def total_of(parts):
    main, extra = parts[0:8, :], parts[8:10, :]
    for n in range(10, parts.shape[0], 10):
        main = main + parts[n : n + 8, :]
        extra = extra + parts[n + 8 : n + 10, :]
    return main, extra


def middle_kernel(parts, out):
    main, extra = total_of(parts)
    for n in range(0, out.shape[0], 10):
        out[n : n + 8, :] = main
        out[n + 8 : n + 10, :] = extra


def solve_kernel(parts, out):
    main, extra = total_of(parts)
    rest = jnp.concatenate([extra if m == 0 else pltpu.roll(extra, 128 - 32 * m, 1) for m in range(4)], axis=0)
    lane8 = iota((8, LANES), 1)
    turns = ((main, 0, 96), (main, 96, 64), (rest, 16, 32), (main, 120, 88))
    pieces = []
    for p, (source, near, far) in enumerate(turns):
        near = pltpu.roll(source, near, 1) if near else source
        piece = jnp.where(lane8 < 32, near, pltpu.roll(source, far, 1))
        pieces.append(jnp.where((lane8 < 64) & ((lane8 & 31) >= 8 * p), piece, 0.0))
    matrix = jnp.concatenate(pieces, axis=0)
    lane = iota((ROWS, LANES), 1)
    half = lane < 32
    turned = jnp.concatenate([matrix, jnp.zeros((LANES - ROWS, LANES), jnp.float32)], axis=0).T
    turned = jnp.where(half, turned[0:ROWS], pltpu.roll(turned[ROWS : 2 * ROWS], 32, 1))
    below = (lane < 64) & (((lane & 31) >> 3) < (iota((ROWS, LANES), 0) >> 3))
    matrix = jnp.where(below, turned, matrix)
    row_lane = iota((1, LANES), 1)
    order = basis_rows()
    for start in range(0, len(order), SOLVE_BLOCK):
        block = order[start : start + SOLVE_BLOCK]
        columns = [jnp.where(half, matrix[:, k : k + 1], matrix[:, 32 + k : 33 + k]) for k in block]
        for j, k in enumerate(block):
            scaled = columns[j] / jnp.broadcast_to(columns[j][k : k + 1, :], (ROWS, LANES))
            for i in range(j + 1, len(block)):
                columns[i] = columns[i] - scaled * columns[i][k : k + 1, :]
            matrix = jnp.where((lane & 31) == k, scaled, matrix - scaled * matrix[k : k + 1, :])
    answer = matrix[SCIENCE_ROW : SCIENCE_ROW + 1, :]
    valid = row_lane < 0
    for k in basis_rows():
        valid = valid | ((row_lane & 31) == k)
    answer = jnp.where(valid & (row_lane < 64), answer, 0.0)
    for n in range(out.shape[0]):
        out[n] = answer


def model_kernel(details, answers, images, model, wide, sums):
    turned = jnp.concatenate([answers[...], jnp.zeros((LANES - 8, LANES), jnp.float32)], axis=0).T
    for v in range(VIS_DEV):
        piece = turned[(v % 2) * ROWS : (v % 2) * ROWS + ROWS, v // 2 : v // 2 + 1]
        wide[v] = jnp.broadcast_to(piece, (ROWS, LANES))
    block = 16

    def step(g, carry):
        near = images.at[pl.ds(pl.multiple_of(g * block * ROWS, block * ROWS), block * ROWS), :]
        for t in range(block):
            v = details[t % 2, 0, g * (block // 2) + t // 2]
            scale = [wide[v, 8 * m : 8 * m + 8] for m in range(4)]
            first = t * ROWS
            for i in range(2):
                lanes = slice(i * LANES, (i + 1) * LANES)
                acc = scale[0] * near[first : first + 8, lanes]
                for m in range(1, 4):
                    acc = acc + scale[m] * near[first + 8 * m : first + 8 * m + 8, lanes]
                sums[(2 * t + i) * 8 : (2 * t + i) * 8 + 8, :] = acc
        out = sums[pl.ds(0, 2 * block, stride=8), :]
        for n in range(1, 8):
            out = out + sums[pl.ds(n, 2 * block, stride=8), :]
        model[pl.ds(pl.multiple_of(g * 2 * block, 2 * block), 2 * block), :] = out.astype(jnp.bfloat16)
        return carry

    lax.fori_loop(0, 2 * LANES // block, step, 0)


def order_kernel(answers, out):
    row, place = iota((LANES, NB), 0), iota((LANES, NB), 1)
    for h in range(2):
        chosen = row < 0
        for k, at in enumerate(basis_rows()):
            chosen = chosen | ((place == k) & (row == 32 * h + at))
        out[pl.ds(h, 8, stride=2), :] = jnp.dot(
            answers[...], jnp.where(chosen, 1.0, 0.0), precision=lax.Precision.HIGHEST,
            preferred_element_type=jnp.float32)


def final_kernel(slots, science, returned, out):
    column = jnp.broadcast_to(slots[0:1, :], (LANES, LANES)).T
    column = jnp.concatenate([column] * 4, axis=1)
    for i in range(2):
        chosen = iota((LANES, 4 * LANES), 1) == column * 2 + i
        chosen = jnp.where(chosen, 1.0, 0.0).astype(jnp.bfloat16)
        model = jnp.dot(chosen, returned[...], preferred_element_type=jnp.float32)
        out[pl.ds(i, LANES, stride=2), :] = science[pl.ds(i, LANES, stride=2), :] - model


def vmem(count):
    return [pl.BlockSpec(memory_space=pltpu.VMEM)] * count


def shape(dims, dtype=jnp.float32):
    return jax.ShapeDtypeStruct(dims, dtype)


def params(mebibytes):
    return pltpu.CompilerParams(vmem_limit_bytes=mebibytes << 20)


def pack(science, sigma, dest, visit, offsets):
    return pl.pallas_call(
        pack_kernel,
        out_shape=(shape((LANES * SLOT_ROWS, LANES), jnp.bfloat16), shape((8, LANES), jnp.int32)),
        in_specs=vmem(5), out_specs=tuple(vmem(2)),
        scratch_shapes=[pltpu.VMEM((5 * LANES, LANES), jnp.bfloat16)],
        compiler_params=params(60), name="pack",
    )(science, sigma, dest, visit, offsets)


def keep(place, parts, tables):
    return pl.pallas_call(
        keep_kernel,
        out_shape=(shape((256, 1024), jnp.bfloat16),) + tuple(shape(t.shape, t.dtype) for t in tables),
        in_specs=[pl.BlockSpec(memory_space=pltpu.SMEM)] + vmem(7), out_specs=tuple(vmem(4)),
        compiler_params=params(8), name="keep",
    )(place, *parts, *tables)


def fit(arrived, template, band, wide_p, wide_q):
    return pl.pallas_call(
        fit_kernel,
        out_shape=(shape((2 * LANES * ROWS, 2 * LANES)), shape((VIS_DEV * 5, LANES)),
                   shape((2, 8, LANES), jnp.int32)),
        in_specs=vmem(5), out_specs=tuple(vmem(3)),
        scratch_shapes=[
            pltpu.VMEM((236 * 9 * 2, 16, LANES), jnp.bfloat16),
            pltpu.VMEM((LANES * SLOT_ROWS, LANES), jnp.float32),
            pltpu.VMEM((2, GROUP * 16, 256), jnp.bfloat16), pltpu.VMEM((2, GROUP * 16, 256), jnp.bfloat16),
            pltpu.VMEM((2, GROUP * 16, len(COLS_P) * LANES), jnp.float32),
            pltpu.VMEM((2, GROUP * 16, len(COLS_Q) * LANES), jnp.float32),
            pltpu.VMEM((2, GROUP * ROWS, 256), jnp.bfloat16),
            pltpu.VMEM((VIS_DEV, ROWS, LANES), jnp.float32),
            pltpu.SMEM((2, 8, LANES), jnp.int32), pltpu.SemaphoreType.DMA,
        ],
        compiler_params=params(40), name="fit",
    )(arrived, template, band, wide_p, wide_q)


def middle(parts):
    return pl.pallas_call(middle_kernel, out_shape=shape((2 * parts.shape[0], LANES)),
                          in_specs=vmem(1), out_specs=vmem(1)[0], compiler_params=params(4), name="middle")(parts)


def solve(parts):
    return pl.pallas_call(solve_kernel, out_shape=shape((8, 1, LANES)),
                          in_specs=vmem(1), out_specs=vmem(1)[0], compiler_params=params(4), name="solve")(parts)


def model_of(details, answers, images):
    return pl.pallas_call(
        model_kernel,
        out_shape=shape((4 * LANES, LANES), jnp.bfloat16),
        in_specs=[pl.BlockSpec(memory_space=pltpu.SMEM)] + vmem(2),
        out_specs=vmem(1)[0],
        scratch_shapes=[pltpu.VMEM((VIS_DEV, ROWS, LANES), jnp.float32),
                        pltpu.VMEM((16 * 16, LANES), jnp.float32)],
        compiler_params=params(14), name="model",
    )(details, answers, images)


def order(answers):
    return pl.pallas_call(order_kernel, out_shape=shape((VIS_DEV, NB)), in_specs=vmem(1),
                          out_specs=vmem(1)[0], compiler_params=params(4), name="order")(answers)


def final(slots, science, returned):
    return pl.pallas_call(final_kernel, out_shape=shape((2 * LANES, LANES)),
                          in_specs=vmem(3), out_specs=vmem(1)[0], compiler_params=params(4), name="final")(slots, science, returned)


def exchange(values, groups=None):
    return lax.all_to_all(values, "patch", split_axis=0, concat_axis=0, tiled=True,
                          axis_index_groups=groups)


def per_device(science, inverse_sigma, template, destination, offsets, visit_local):
    patches = lax.axis_size("patch")
    planes = [[z * 8 + i for i in range(8)] for z in range(patches // 8)]
    lines = [[z * 8 + i for z in range(patches // 8)] for i in range(8)]
    own = template[0].astype(jnp.bfloat16)
    parts = [own] + [lax.ppermute(own, "visit", [(x, x ^ m) for x in range(4)]) for m in (1, 2, 3)]
    place = lax.axis_index("visit").astype(jnp.int32).reshape(1)
    science_rows = science.reshape(2 * LANES, LANES)
    packed, slots = pack(science_rows, inverse_sigma.reshape(2 * LANES, LANES),
                         destination.reshape(1, LANES), visit_local.reshape(1, LANES), offsets.T)
    kept = keep(place, parts, constants())
    arrived = exchange(packed.reshape(patches, 5, 2, LANES)).reshape(LANES * SLOT_ROWS, LANES)
    images, gram, details = fit(arrived, *kept)
    parts = exchange(gram.reshape(8, 5, 2, LANES), planes).reshape(gram.shape)
    parts = exchange(middle(parts).reshape(16, 5, 2, LANES), lines).reshape(160, LANES)
    answers = exchange(solve(parts), planes).reshape(8, LANES)
    model = model_of(details, answers, images)
    returned = exchange(model.reshape(patches, 2, 2, LANES)).reshape(4 * LANES, LANES)
    difference = final(slots, science_rows, returned)
    coefficients = order(answers)
    return difference.reshape(science.shape), coefficients


def solution(mesh):
    return jax.shard_map(
        per_device,
        mesh=mesh,
        in_specs=(
            P(("patch", "visit"), None, None),
            P(("patch", "visit"), None, None),
            P("patch", "visit", None),
            P(("patch", "visit")),
            P(("patch", "visit"), None),
            P(("patch", "visit")),
        ),
        out_specs=(P(("patch", "visit"), None, None), P("visit", None)),
        check_vma=False,
    )
```
